32 devices in a mesh: dp: 8 (over y, x, core), vit: 4 (over z).
Axes of the slice: x: 2, y: 2, z: 4, core: 2. Of those that a mesh axis runs over, the one named last changes fastest.
Arguments:
- patch_states: bfloat16 [8192, 1280], P(('dp', 'vit')), may hold values from -1 to 1, as said below
- queries: bfloat16 [8192, 1280], P(('dp', 'vit')), may hold values from -128 to 128
- keys: bfloat16 [8192, 1280], P(('dp', 'vit')), may hold values from -4 to 4
- values: bfloat16 [8192, 1280], P(('dp', 'vit')), may hold values from -6 to 6
- out_proj: bfloat16 [1280, 1280], replicated, may hold values from -0.15625 to 0.15625
- merge_gain: float32 [1280], replicated, may hold values from 0.1 to 1.9
- image_of_group: int32 [8, 256], P('dp'), may hold values from 0 to 5, never falling along the last dimension, each value on 1 to 160 neighbouring positions
- w_in: bfloat16 [5120, 5120], P('dp', 'vit'), may hold values from -0.078125 to 0.078125
- w_out: bfloat16 [8192, 5120], P('dp', 'vit'), may hold values from -0.078125 to 0.078125
- text_embeds: bfloat16 [4096, 8192], P(('dp', 'vit')), may hold values from -6 to 6
- block_dest: int32 [32, 8], P(('dp', 'vit')), may hold values from 0 to 7, as said below
- placeholder_rows: int32 [32, 16], P(('dp', 'vit')), may hold values from -1 to 120, as said below
Outputs:
- merged_text: bfloat16 [4096, 8192], P(('dp', 'vit'))
The draws below stay inside these ranges and needn't reach their ends.
Inputs may be any that keep to these rules, and one draw needn't show every extreme that they name: `patch_states`: row scales of one draw differ from row to row. `block_dest`: A device sends at most 2 of its blocks to one index of dp. `placeholder_rows`: entry 2 d + k of text shard s is set exactly when the device of index d along dp and of s's index along vit sends s a block with slot_rank k; then it is a multiple of 8, and the 8 rows from it of all blocks arriving at s are disjoint; else it is -1.
All inputs are finite; a program needn't handle non-finite values.
Results may differ from the reference program's by a relative error of at most 0.008.
Values may be sent and summed in bfloat16 or wider, within the bound.
No kernel may reach another device: no remote copies, remote signals or barrier semaphores. Data moves between devices by JAX's collectives and lax.ppermute only.
A program may use at most 192 MiB of HBM per device.

```python
import math
import jax
import jax.numpy as jnp
import numpy as np
from jax import lax

WIDTH = 1280
HEADS = 16
HEAD_DIM = 80
MERGE_HID = 5120
LM_WIDTH = 8192
TEXT_DEV = 128
IMAGES = 6
BLOCKS_DEV = 8
BLOCK_ROWS = 8
GROUP = 1024
PATCHES = 8192
MOST_GROUPS = 160
TEXT_ROWS = 4096
N_DP = 8
N_VIT = 4
DEVICES = 32


def drawn_pair(key):
    base_key = jax.random.fold_in(key, 701)
    key_draw = jnp.clip(jax.random.normal(jax.random.fold_in(base_key, 1), (PATCHES, WIDTH), jnp.float32), -4.0, 4.0)
    query_draw = jnp.clip(jax.random.normal(jax.random.fold_in(base_key, 2), (PATCHES, WIDTH), jnp.float32), -4.0, 4.0)
    return (query_draw, key_draw)


def draw_queries(key, part):
    return drawn_pair(key)[0].astype(jnp.bfloat16)


def draw_keys(key, part):
    return drawn_pair(key)[1].astype(jnp.bfloat16)


def draw_patch_states(key, part):
    base_key = jax.random.fold_in(key, 809)
    entries = jnp.clip(jax.random.normal(jax.random.fold_in(base_key, 1), (PATCHES, WIDTH), jnp.float32), -4.0, 4.0)
    scales = 0.02 * jnp.exp(jax.random.uniform(jax.random.fold_in(base_key, 2), (PATCHES, 1), jnp.float32, 0.0, math.log(10.0)))
    return (entries * scales).astype(jnp.bfloat16)


def routing(key):
    base_key = jax.random.fold_in(key, 303)
    crowded = jax.random.randint(jax.random.fold_in(base_key, 1), (N_VIT, 1, 1), 0, N_DP)
    rank_keys = jax.random.randint(jax.random.fold_in(base_key, 2), (N_VIT, N_DP, N_DP - 1), 0, 1 << 20) * N_DP + jnp.arange(N_DP - 1, dtype=jnp.int32)
    others = jnp.argsort(rank_keys, axis=-1).astype(jnp.int32) + 1
    ordering = jnp.concatenate([jnp.zeros((N_VIT, N_DP, 1), jnp.int32), others], axis=-1)
    ordering = (ordering + crowded) % N_DP
    block_keys = jax.random.randint(jax.random.fold_in(base_key, 3), (N_VIT, N_DP, BLOCKS_DEV), 0, 1 << 20) * BLOCKS_DEV + jnp.arange(BLOCKS_DEV, dtype=jnp.int32)
    shuffle = jnp.argsort(block_keys, axis=-1).astype(jnp.int32)
    targets = jnp.take_along_axis(ordering, shuffle // 2, axis=-1).astype(jnp.int32)
    positions = jnp.arange(BLOCKS_DEV, dtype=jnp.int32)
    repeats = (targets[..., :, None] == targets[..., None, :]) & (positions[None, :] < positions[:, None])
    slot_rank = jnp.sum(repeats.astype(jnp.int32), axis=-1).astype(jnp.int32)
    arrivals = (targets[..., None, None] == jnp.arange(N_DP, dtype=jnp.int32)[:, None]) & (slot_rank[..., None, None] == jnp.arange(2, dtype=jnp.int32)[None, :])
    present = jnp.any(arrivals, axis=2)
    present = jnp.transpose(present, (0, 2, 1, 3)).reshape(N_VIT, N_DP, 2 * N_DP).astype(jnp.int32)
    ranking = (jnp.cumsum(present, axis=-1) - present).astype(jnp.int32)
    spot_count = TEXT_DEV // BLOCK_ROWS
    spot_keys = jax.random.randint(jax.random.fold_in(base_key, 4), (N_VIT, N_DP, spot_count), 0, 1 << 20) * spot_count + jnp.arange(spot_count, dtype=jnp.int32)
    free_spots = jnp.argsort(spot_keys, axis=-1).astype(jnp.int32)
    offset = jnp.take_along_axis(free_spots, ranking, axis=-1) * BLOCK_ROWS
    offsets_table = jnp.where(present > 0, offset, -1).astype(jnp.int32)
    offsets_table = jnp.transpose(offsets_table, (1, 0, 2)).reshape(DEVICES, 2 * N_DP)
    destination = jnp.transpose(targets, (1, 0, 2)).reshape(DEVICES, BLOCKS_DEV)
    return (destination, offsets_table)


def draw_block_dest(key, part):
    return routing(key)[0]


def draw_placeholder_rows(key, part):
    return routing(key)[1]


def shard_levels(own_key, shape, shards, low, largest):
    loudness, own = 1.0, jax.random.fold_in(own_key, 6)
    for axis_at, shards_of in shards:
        steps = jnp.exp(jax.random.uniform(jax.random.fold_in(own, axis_at), (shards_of,), jnp.float32, low / len(shards), largest / len(shards)))
        loudness = loudness * jnp.repeat(steps, shape[axis_at] // shards_of).reshape([-1 if axis == axis_at else 1 for axis in range(len(shape))])
    return loudness


def profile(amount, total, most, skew):
    weights = [(1 << 20) // math.isqrt(grade ** skew) + 1 for grade in range(2, amount + 1)]
    rest, holding = total - most - (amount - 1), [1] * (amount - 1)
    while rest > 0:
        free = [i for i in range(amount - 1) if holding[i] < most]
        whole, budget = sum([weights[i] for i in free]), rest
        for i in free:
            more = min(most - holding[i], max(1, budget * weights[i] // whole), rest)
            holding[i] = holding[i] + more
            rest = rest - more
    return np.array([most] + holding)


def uneven(own_key, amount, total, limit, lean):
    if amount == 2:
        one = jax.random.randint(own_key, (), max(1, total - limit), min(limit, total - 1) + 1)
        return jnp.stack([one, total - one])
    sizes = jnp.asarray(profile(amount, total, limit, lean), jnp.int32)
    pairs = (amount - 1) // 2
    giver, taker = sizes[1:1 + 2 * pairs:2], sizes[2:2 + 2 * pairs:2]
    room = jnp.minimum(giver - 1, limit - taker)
    passed = jax.random.randint(jax.random.fold_in(own_key, 1), (pairs,), 0, 1 << 20) % (room + 1)
    sizes = sizes.at[1:1 + 2 * pairs:2].set(giver - passed).at[2:2 + 2 * pairs:2].set(taker + passed)
    return sizes[jax.random.permutation(jax.random.fold_in(own_key, 2), amount)]


def bell_draw(rng, shape, spread, most, cuts=(), held_as=jnp.bfloat16):
    values = spread * jax.random.normal(rng, shape, jnp.float32)
    if cuts:
        values = values * shard_levels(rng, shape, cuts, -0.22, 0.18)
    return jnp.clip(values, -most, most).astype(held_as)


def setup_inputs(seed: int = 0) -> dict:
    splits = jax.random.split(jax.random.key(seed), 13)
    patch_states = draw_patch_states(jax.random.fold_in(splits[12], 71), 0)
    queries = draw_queries(jax.random.fold_in(splits[12], 71), 0)
    keys = draw_keys(jax.random.fold_in(splits[12], 71), 0)
    values = bell_draw(splits[3], (PATCHES, WIDTH), 1.0, 6.0, ((0, 32),))
    out_proj = bell_draw(splits[4], (WIDTH, WIDTH), WIDTH ** -0.5, 0.15625)
    merge_gain = jnp.clip(1.0 + 0.18 * jax.random.normal(splits[5], (WIDTH,), jnp.float32), 0.1, 1.9)
    image_of_group = jax.vmap(lambda own: jnp.searchsorted(jnp.cumsum(uneven(own, IMAGES, GROUP // 4, MOST_GROUPS, 2)), jnp.arange(GROUP // 4), side="right"))(jax.random.split(splits[6], N_DP)).reshape((N_DP, GROUP // 4)).astype(jnp.int32)
    w_in = bell_draw(splits[7], (4 * WIDTH, MERGE_HID), (4 * WIDTH) ** -0.5, 0.078125, ((0, 8), (1, 4)))
    w_out = bell_draw(splits[8], (LM_WIDTH, MERGE_HID), MERGE_HID ** -0.5, 0.078125, ((0, 8), (1, 4)))
    text_embeds = bell_draw(splits[9], (TEXT_ROWS, LM_WIDTH), 1.0, 6.0, ((0, 32),))
    block_dest = draw_block_dest(jax.random.fold_in(splits[12], 71), 0)
    placeholder_rows = draw_placeholder_rows(jax.random.fold_in(splits[12], 71), 0)
    return {"patch_states": patch_states, "queries": queries, "keys": keys, "values": values, "out_proj": out_proj, "merge_gain": merge_gain, "image_of_group": image_of_group, "w_in": w_in, "w_out": w_out, "text_embeds": text_embeds, "block_dest": block_dest, "placeholder_rows": placeholder_rows}


EPSILON = 1e-06

def normalize(states, gain_vector):
    mean_square = lax.optimization_barrier(jnp.mean(states * states, axis=-1, keepdims=True))
    return states * lax.rsqrt(mean_square + EPSILON) * gain_vector

def attend(inputs):
    query_rows, key_rows, value_rows, image_ids = inputs
    row_count = query_rows.shape[0]
    query_heads = query_rows.astype(jnp.float32).reshape(row_count, HEADS, HEAD_DIM)
    key_heads = key_rows.astype(jnp.float32).reshape(row_count, HEADS, HEAD_DIM)
    value_heads = value_rows.astype(jnp.float32).reshape(row_count, HEADS, HEAD_DIM)
    scores = jnp.einsum('qhd,khd->hqk', query_heads, key_heads) * HEAD_DIM ** (-0.5)
    allowed = (image_ids[:, None] == image_ids[None, :])[None]
    scores = jnp.where(allowed, scores, -1e+30)
    highest = lax.optimization_barrier(jnp.max(scores, axis=-1, keepdims=True))
    exponent = jnp.where(allowed, jnp.exp(scores - highest), 0.0)
    weights = (exponent / lax.optimization_barrier(jnp.sum(exponent, axis=-1, keepdims=True))).astype(jnp.bfloat16)
    attended = jnp.einsum('hqk,khd->qhd', weights.astype(jnp.float32), value_heads)
    return attended.reshape(row_count, WIDTH).astype(jnp.bfloat16)

def reference(patch_states, queries, keys, values, out_proj, merge_gain, image_of_group, w_in, w_out, text_embeds, block_dest, placeholder_rows):
    image_ids = jnp.repeat(image_of_group, 4, axis=1)
    attended = lax.map(attend, (queries.reshape(N_DP, GROUP, WIDTH), keys.reshape(N_DP, GROUP, WIDTH), values.reshape(N_DP, GROUP, WIDTH), image_ids))
    attended = attended.reshape(PATCHES, WIDTH)
    residual = patch_states.astype(jnp.float32) + jnp.dot(attended, out_proj, preferred_element_type=jnp.float32)
    normed = normalize(residual, merge_gain).astype(jnp.bfloat16)
    merge_rows = normed.reshape(PATCHES // 4, 4 * WIDTH)
    hidden = jax.nn.gelu(jnp.dot(merge_rows, w_in, preferred_element_type=jnp.float32), approximate=False).astype(jnp.bfloat16)
    portion = MERGE_HID // N_VIT
    merged = jnp.zeros((PATCHES // 4, LM_WIDTH), jnp.float32)
    for member in range(N_VIT):
        partial_sum = lax.dot_general(hidden[:, member * portion:(member + 1) * portion], w_out[:, member * portion:(member + 1) * portion], (((1,), (1,)), ((), ())), preferred_element_type=jnp.float32)
        rounded = lax.optimization_barrier(partial_sum.astype(jnp.bfloat16))
        merged = merged + rounded.astype(jnp.float32)
    merged = merged.astype(jnp.bfloat16)
    device_ids = jnp.arange(DEVICES, dtype=jnp.int32)
    sender_dp = device_ids // N_VIT
    sender_vit = device_ids % N_VIT
    positions = jnp.arange(BLOCKS_DEV, dtype=jnp.int32)
    earlier = (block_dest[:, :, None] == block_dest[:, None, :]) & (positions[None, None, :] < positions[None, :, None])
    slot_rank = lax.optimization_barrier(jnp.sum(earlier.astype(jnp.int32), axis=-1)).astype(jnp.int32)
    receiver = (block_dest * N_VIT + sender_vit[:, None]).astype(jnp.int32)
    first_row = placeholder_rows[receiver, (sender_dp[:, None] * 2 + slot_rank).astype(jnp.int32)]
    targets = (receiver * TEXT_DEV + first_row)[:, :, None] + jnp.arange(BLOCK_ROWS, dtype=jnp.int32)[None, None, :]
    return text_embeds.at[targets.reshape(-1).astype(jnp.int32)].set(merged)
```

```python
import functools

import jax
import jax.numpy as jnp
from jax import lax
from jax.experimental import pallas as pl
from jax.experimental.pallas import tpu as pltpu
from jax.sharding import PartitionSpec as P

HEADS = 16
HEAD_DIM = 80
EPSILON = 1e-06
LANES = 128
CHUNKS = 2


def fold_of(width):
    fold = 1
    while (width * fold) % LANES:
        fold *= 2
    return fold


def pack_kernel(members, fold, q_ref, k_ref, v_ref, out_ref):
    rows, width = q_ref.shape
    part, piece = width // members, rows // fold
    for at, ref in enumerate((q_ref, k_ref, v_ref)):
        for member in range(members):
            for turn in range(fold):
                out_ref[member, at, :, turn * part : (turn + 1) * part] = ref[
                    turn * piece : (turn + 1) * piece, member * part : (member + 1) * part
                ]


def attend_kernel(heads, fold, ids_col_ref, ids_row_ref, packed_ref, out_ref, q_buf, k_buf, v_buf):
    members, _, piece, _ = packed_ref.shape
    part = heads * HEAD_DIM
    tiles = members * fold
    lane = lax.broadcasted_iota(jnp.int32, (piece, LANES - HEAD_DIM), 1)
    ones = jnp.where(lane == 0, 1.0, 0.0).astype(jnp.bfloat16)
    zeros = jnp.zeros((piece, LANES - HEAD_DIM), jnp.bfloat16)
    for head in range(heads):
        for turn in range(fold):
            low = turn * part + head * HEAD_DIM
            for member in range(members):
                rows = slice((member * fold + turn) * piece, (member * fold + turn + 1) * piece)
                q_buf[head, rows, :HEAD_DIM] = packed_ref[member, 0, :, low : low + HEAD_DIM]
                k_buf[head, rows, :HEAD_DIM] = packed_ref[member, 1, :, low : low + HEAD_DIM]
                v_buf[head, rows, :HEAD_DIM] = packed_ref[member, 2, :, low : low + HEAD_DIM]
                q_buf[head, rows, HEAD_DIM:] = zeros
                k_buf[head, rows, HEAD_DIM:] = zeros
                v_buf[head, rows, HEAD_DIM:] = ones

    def one_member(member, carry):
        for turn in range(fold):
            start = pl.multiple_of((member * fold + turn) * piece, piece)
            rows = pl.ds(start, piece)
            allowed = ids_col_ref[rows, :] == ids_row_ref[...]
            for head in range(heads):
                scores = lax.dot_general(
                    q_buf[head, rows, :],
                    k_buf[head],
                    (((1,), (1,)), ((), ())),
                    preferred_element_type=jnp.float32,
                )
                scores = jnp.where(allowed, scores, -1e30)
                highest = jnp.max(scores, axis=-1, keepdims=True)
                weights = jnp.exp((scores - highest) * HEAD_DIM ** (-0.5)).astype(jnp.bfloat16)
                mixed = jnp.dot(weights, v_buf[head], preferred_element_type=jnp.float32)
                mixed = mixed[:, :HEAD_DIM] / mixed[:, HEAD_DIM : HEAD_DIM + 1]
                low = turn * part + head * HEAD_DIM
                out_ref[member, :, low : low + HEAD_DIM] = mixed.astype(jnp.bfloat16)
        return carry

    lax.fori_loop(0, members, one_member, 0)


def project_kernel(fold, packed_ref, patch_ref, proj_ref, gain_ref, out_ref, rows_buf):
    members, piece, wide = packed_ref.shape
    part = wide // fold
    for member in range(members):
        for turn in range(fold):
            rows_buf[turn * piece : (turn + 1) * piece, member * part : (member + 1) * part] = (
                packed_ref[member, :, turn * part : (turn + 1) * part]
            )
    residual = patch_ref[...].astype(jnp.float32) + jnp.dot(
        rows_buf[...], proj_ref[...], preferred_element_type=jnp.float32
    )
    mean_square = jnp.mean(residual * residual, axis=-1, keepdims=True)
    out_ref[...] = (residual * lax.rsqrt(mean_square + EPSILON) * gain_ref[...]).astype(
        jnp.bfloat16
    )


def ring(value, step):
    members = lax.axis_size("vit")
    return lax.ppermute(value, "vit", [(i, (i + step) % members) for i in range(members)])


def body(
    patch_states,
    queries,
    keys,
    values,
    out_proj,
    merge_gain,
    image_of_group,
    w_in,
    w_out,
    text_embeds,
    block_dest,
    placeholder_rows,
):
    row_count, feature_width = queries.shape
    members = lax.axis_size("vit")
    part = feature_width // members
    heads = HEADS // members
    fold = fold_of(part)
    piece = row_count // fold
    group = row_count * members

    up_full = lax.all_gather(w_in, "dp", axis=0, tiled=True)
    out_rows = w_out.shape[0]
    senders = lax.axis_size("dp")
    down_parts = [
        lax.all_gather(
            w_out[c * (out_rows // CHUNKS) : (c + 1) * (out_rows // CHUNKS)], "dp", axis=0, tiled=True
        )
        for c in range(CHUNKS)
    ]

    packed = pl.pallas_call(
        functools.partial(pack_kernel, members, fold),
        out_shape=jax.ShapeDtypeStruct((members, 3, piece, part * fold), jnp.bfloat16),
        name="pack",
    )(queries, keys, values)
    packed = lax.all_to_all(packed, "vit", split_axis=0, concat_axis=0, tiled=True)

    image_ids = jnp.repeat(image_of_group[0], 4)
    attended = pl.pallas_call(
        functools.partial(attend_kernel, heads, fold),
        out_shape=jax.ShapeDtypeStruct((members, piece, part * fold), jnp.bfloat16),
        scratch_shapes=[pltpu.VMEM((heads, group, LANES), jnp.bfloat16)] * 3,
        name="attend",
    )(image_ids[:, None], image_ids[None, :], packed)
    attended = lax.all_to_all(attended, "vit", split_axis=0, concat_axis=0, tiled=True)

    normed = pl.pallas_call(
        functools.partial(project_kernel, fold),
        out_shape=jax.ShapeDtypeStruct((row_count, feature_width), jnp.bfloat16),
        scratch_shapes=[pltpu.VMEM((row_count, feature_width), jnp.bfloat16)],
        name="project",
    )(attended, patch_states, out_proj, merge_gain[None, :])
    merge_rows = normed.reshape(row_count // 4, 4 * feature_width)

    half = merge_rows.shape[0] // 2
    above, below = merge_rows[:half], merge_rows[half:]
    up_blocks, down_blocks = {0: above}, {0: below}
    for step in range(1, members):
        above = ring(above, 1)
        below = ring(below, -1)
        up_blocks[members - step] = above
        down_blocks[step] = below
    group_rows = jnp.concatenate(
        [up_blocks[i] for i in range(members)] + [down_blocks[i] for i in range(members)], axis=0
    )
    hidden = jax.nn.gelu(
        jnp.dot(group_rows, up_full, preferred_element_type=jnp.float32), approximate=False
    ).astype(jnp.bfloat16)

    blocks = block_dest.shape[1]
    block_height = merge_rows.shape[0] // blocks
    destination = block_dest[0]
    positions = jnp.arange(blocks, dtype=jnp.int32)
    earlier = (destination[:, None] == destination[None, :]) & (
        positions[None, :] < positions[:, None]
    )
    slot_rank = jnp.sum(earlier.astype(jnp.int32), axis=1)
    slot_index = destination * 2 + slot_rank
    row_slots = (
        slot_index[:, None] * block_height + jnp.arange(block_height, dtype=jnp.int32)[None, :]
    ).reshape(-1)
    slots = 2 * senders * block_height
    selector = (jnp.arange(slots, dtype=jnp.int32)[:, None] == row_slots[None, :]).astype(
        jnp.bfloat16
    )
    first_row = placeholder_rows[0]
    targets = jnp.where(
        first_row[:, None] >= 0,
        first_row[:, None] + jnp.arange(block_height, dtype=jnp.int32)[None, :],
        -1,
    ).reshape(-1)
    placement = jnp.arange(text_embeds.shape[0], dtype=jnp.int32)[:, None] == targets[None, :]
    covered = jnp.any(placement, axis=1)
    placement = placement.astype(jnp.bfloat16)

    arrived = []
    for c in range(CHUNKS):
        partial_sum = lax.dot_general(
            hidden, down_parts[c], (((1,), (1,)), ((), ())), preferred_element_type=jnp.float32
        ).astype(jnp.bfloat16)
        held = partial_sum.reshape(2, members, half, partial_sum.shape[1])
        plus, minus = held[0, members - 1], held[1, 1]
        for step in range(1, members):
            plus = ring(plus, 1).astype(jnp.float32) + held[0, members - 1 - step].astype(
                jnp.float32
            )
            minus = ring(minus, -1).astype(jnp.float32) + held[1, (1 + step) % members].astype(
                jnp.float32
            )
            plus, minus = plus.astype(jnp.bfloat16), minus.astype(jnp.bfloat16)
        merged = jnp.concatenate([plus, minus], axis=0)
        outgoing = jnp.dot(selector, merged, preferred_element_type=jnp.float32).astype(
            jnp.bfloat16
        )
        outgoing = outgoing.reshape(senders, 2 * block_height, merged.shape[1])
        incoming = lax.all_to_all(outgoing, "dp", split_axis=0, concat_axis=0, tiled=True)
        arrived.append(incoming.reshape(slots, merged.shape[1]))

    wide = out_rows // CHUNKS
    text = text_embeds.reshape(text_embeds.shape[0], senders, CHUNKS, wide)
    pieces = []
    for c in range(CHUNKS):
        placed = jnp.dot(placement, arrived[c], preferred_element_type=jnp.float32).astype(
            jnp.bfloat16
        )
        placed = placed.reshape(text_embeds.shape[0], senders, wide)
        pieces.append(jnp.where(covered[:, None, None], placed, text[:, :, c]))
    return jnp.stack(pieces, axis=2).reshape(text_embeds.shape)


def solution(mesh):
    placed = (
        P(("dp", "vit"), None),
        P(("dp", "vit"), None),
        P(("dp", "vit"), None),
        P(("dp", "vit"), None),
        P(),
        P(),
        P("dp", None),
        P("dp", "vit"),
        P("dp", "vit"),
        P(("dp", "vit"), None),
        P(("dp", "vit"), None),
        P(("dp", "vit"), None),
    )
    return jax.shard_map(
        body, mesh=mesh, in_specs=placed, out_specs=P(("dp", "vit"), None), check_vma=False
    )
```

```python
import functools

import jax
import jax.numpy as jnp
from jax import lax
from jax.experimental import pallas as pl
from jax.experimental.pallas import tpu as pltpu
from jax.sharding import PartitionSpec as P

HEADS = 16
HEAD_DIM = 80
EPSILON = 1e-06
LANES = 128
CHUNKS = 2


def fold_of(width):
    fold = 1
    while (width * fold) % LANES:
        fold *= 2
    return fold


def pack_kernel(members, fold, q_ref, k_ref, v_ref, out_ref):
    rows, width = q_ref.shape
    part, piece = width // members, rows // fold
    for at, ref in enumerate((q_ref, k_ref, v_ref)):
        for member in range(members):
            for turn in range(fold):
                out_ref[member, at, :, turn * part : (turn + 1) * part] = ref[
                    turn * piece : (turn + 1) * piece, member * part : (member + 1) * part
                ]


def attend_kernel(heads, fold, ids_col_ref, ids_row_ref, packed_ref, out_ref, q_buf, k_buf, v_buf):
    members, _, piece, _ = packed_ref.shape
    part = heads * HEAD_DIM
    tiles = members * fold
    lane = lax.broadcasted_iota(jnp.int32, (piece, LANES - HEAD_DIM), 1)
    ones = jnp.where(lane == 0, 1.0, 0.0).astype(jnp.bfloat16)
    zeros = jnp.zeros((piece, LANES - HEAD_DIM), jnp.bfloat16)
    for head in range(heads):
        for turn in range(fold):
            low = turn * part + head * HEAD_DIM
            for member in range(members):
                rows = slice((member * fold + turn) * piece, (member * fold + turn + 1) * piece)
                q_buf[head, rows, :HEAD_DIM] = packed_ref[member, 0, :, low : low + HEAD_DIM]
                k_buf[head, rows, :HEAD_DIM] = packed_ref[member, 1, :, low : low + HEAD_DIM]
                v_buf[head, rows, :HEAD_DIM] = packed_ref[member, 2, :, low : low + HEAD_DIM]
                q_buf[head, rows, HEAD_DIM:] = zeros
                k_buf[head, rows, HEAD_DIM:] = zeros
                v_buf[head, rows, HEAD_DIM:] = ones

    def one_member(member, carry):
        for turn in range(fold):
            start = pl.multiple_of((member * fold + turn) * piece, piece)
            rows = pl.ds(start, piece)
            allowed = ids_col_ref[rows, :] == ids_row_ref[...]
            for head in range(heads):
                scores = lax.dot_general(
                    q_buf[head, rows, :],
                    k_buf[head],
                    (((1,), (1,)), ((), ())),
                    preferred_element_type=jnp.float32,
                )
                scores = jnp.where(allowed, scores, -1e30)
                highest = jnp.max(scores, axis=-1, keepdims=True)
                weights = jnp.exp((scores - highest) * HEAD_DIM ** (-0.5)).astype(jnp.bfloat16)
                mixed = jnp.dot(weights, v_buf[head], preferred_element_type=jnp.float32)
                mixed = mixed[:, :HEAD_DIM] / mixed[:, HEAD_DIM : HEAD_DIM + 1]
                low = turn * part + head * HEAD_DIM
                out_ref[member, :, low : low + HEAD_DIM] = mixed.astype(jnp.bfloat16)
        return carry

    lax.fori_loop(0, members, one_member, 0)


def project_kernel(fold, packed_ref, patch_ref, proj_ref, gain_ref, out_ref, rows_buf):
    members, piece, wide = packed_ref.shape
    part = wide // fold
    for member in range(members):
        for turn in range(fold):
            rows_buf[turn * piece : (turn + 1) * piece, member * part : (member + 1) * part] = (
                packed_ref[member, :, turn * part : (turn + 1) * part]
            )
    residual = patch_ref[...].astype(jnp.float32) + jnp.dot(
        rows_buf[...], proj_ref[...], preferred_element_type=jnp.float32
    )
    mean_square = jnp.mean(residual * residual, axis=-1, keepdims=True)
    out_ref[...] = (residual * lax.rsqrt(mean_square + EPSILON) * gain_ref[...]).astype(
        jnp.bfloat16
    )


def hidden_kernel(pieces, more, members, me_ref, *refs):
    blocks, refs = refs[: 2 * members], refs[2 * members :]
    first, refs = refs[: len(pieces)], refs[len(pieces) :]
    second, refs = refs[: len(more)], refs[len(more) :]
    hidden_ref, refs = refs[0], refs[1:]
    sums, refs = refs[: 2 * members], refs[2 * members :]
    rows_buf, up_buf, down_buf, acc, up_sem, down_sem = refs
    fetch(pieces, first, up_buf, up_sem)
    fetch(more, second, down_buf, down_sem)
    count, _, depth = rows_buf.shape
    half = blocks[0].shape[0]
    for at, block in enumerate(blocks):
        for k in range(count):
            rows_buf[k, at * half : (at + 1) * half, :] = block[:, k * depth : (k + 1) * depth]
    acc[...] = jnp.zeros_like(acc)

    def one_piece(mask, carry):
        arrive(up_buf, up_sem, mask)
        acc[...] += jnp.dot(
            rows_buf[me_ref[0] ^ mask], up_buf[mask], preferred_element_type=jnp.float32
        )
        return carry

    lax.fori_loop(0, count, one_piece, 0)
    total = acc[...]
    hidden_ref[...] = (0.5 * total * (1.0 + lax.erf(total * 0.5**0.5))).astype(jnp.bfloat16)
    contract(me_ref, hidden_ref, down_buf, down_sem, sums)


def sums_kernel(pieces, members, me_ref, hidden_ref, *refs):
    given, refs = refs[: len(pieces)], refs[len(pieces) :]
    sums, refs = refs[: 2 * members], refs[2 * members :]
    down_buf, down_sem = refs
    fetch(pieces, given, down_buf, down_sem)
    contract(me_ref, hidden_ref, down_buf, down_sem, sums)


def fetch(pieces, refs, buf, sem):
    for (mask, low, length), ref in zip(pieces, refs):
        pltpu.make_async_copy(ref, buf.at[mask, pl.ds(low, length)], sem.at[mask]).start()


def arrive(buf, sem, mask):
    pltpu.make_async_copy(buf.at[mask], buf.at[mask], sem.at[mask]).wait()


def contract(me_ref, hidden_ref, down_buf, down_sem, sums):
    count, wide, _ = down_buf.shape
    half = sums[0].shape[0]

    def one_piece(mask, carry):
        arrive(down_buf, down_sem, mask)
        product = lax.dot_general(
            hidden_ref[...],
            down_buf[mask],
            (((1,), (1,)), ((), ())),
            preferred_element_type=jnp.float32,
        ).astype(jnp.bfloat16)
        low = pl.multiple_of((me_ref[0] ^ mask) * wide, wide)
        for at, ref in enumerate(sums):
            ref[:, pl.ds(low, wide)] = product[at * half : (at + 1) * half]
        return carry

    lax.fori_loop(0, count, one_piece, 0)


def route_kernel(selector_ref, plus_ref, plus_own_ref, minus_ref, minus_own_ref, out_ref):
    plus = plus_ref[...].astype(jnp.float32) + plus_own_ref[...].astype(jnp.float32)
    minus = minus_ref[...].astype(jnp.float32) + minus_own_ref[...].astype(jnp.float32)
    merged = jnp.concatenate([plus.astype(jnp.bfloat16), minus.astype(jnp.bfloat16)], axis=0)
    out_ref[...] = jnp.dot(
        selector_ref[...], merged, preferred_element_type=jnp.float32
    ).astype(jnp.bfloat16)


def place_kernel(count, covered_ref, placement_ref, text_ref, *refs):
    arrived, out_ref = refs[:-1], refs[-1]
    covered = covered_ref[...] > 0
    step = text_ref.shape[1] // count
    wide = step // len(arrived)

    def one_block(at, carry):
        for c, ref in enumerate(arrived):
            source = pl.ds(pl.multiple_of(at * wide, wide), wide)
            target = pl.ds(pl.multiple_of(at * step + c * wide, wide), wide)
            placed = jnp.dot(
                placement_ref[...], ref[:, source], preferred_element_type=jnp.float32
            ).astype(jnp.bfloat16)
            out_ref[:, target] = jnp.where(covered, placed, text_ref[:, target])
        return carry

    lax.fori_loop(0, count, one_block, 0)


def ring(value, step):
    members = lax.axis_size("vit")
    return lax.ppermute(value, "vit", [(i, (i + step) % members) for i in range(members)])


def gather_pieces(value):
    senders, rows = lax.axis_size("dp"), value.shape[0]
    side = 1
    while 2 * side * side < senders:
        side *= 2
    along_x, along_y = 2 * (side - 1), 2 * side * (side - 1)
    unit = 128 if rows >= 256 else 16
    cut = rows // 2 // unit * unit

    def swap(array, mask):
        return lax.ppermute(array, "dp", [(i, i ^ mask) for i in range(senders)])

    def part_of(parts, top):
        if len(parts) == 2:
            return parts[0 if top else 1]
        array = parts[0][1]
        return (0, array[:cut]) if top else (cut, array[cut:])

    def high(mask):
        return 1 << (mask.bit_length() - 1)

    found = {0: [(0, value)]}
    for mask in range(2, senders, 2):
        x, y = mask & along_x, mask & along_y
        if x and y:
            top = part_of(found[x | (y ^ high(y))], True)
            bottom = part_of(found[(x ^ high(x)) | y], False)
            found[mask] = [
                (top[0], swap(top[1], high(y))),
                (bottom[0], swap(bottom[1], high(x))),
            ]
        else:
            found[mask] = [(low, swap(a, high(mask))) for low, a in found[mask ^ high(mask)]]
    for mask in range(1, senders, 2):
        found[mask] = [(low, swap(a, 1)) for low, a in found[mask ^ 1]]
    order = [(mask, low, a) for mask in range(senders) for low, a in found[mask]]
    return [(mask, low, a.shape[0]) for mask, low, a in order], [a for _, _, a in order]


def body(
    patch_states,
    queries,
    keys,
    values,
    out_proj,
    merge_gain,
    image_of_group,
    w_in,
    w_out,
    text_embeds,
    block_dest,
    placeholder_rows,
):
    row_count, feature_width = queries.shape
    members = lax.axis_size("vit")
    senders = lax.axis_size("dp")
    me = lax.axis_index("dp").astype(jnp.int32)[None]
    part = feature_width // members
    heads = HEADS // members
    fold = fold_of(part)
    piece = row_count // fold
    group = row_count * members
    vmem = pl.BlockSpec(memory_space=pltpu.VMEM)
    smem = pl.BlockSpec(memory_space=pltpu.SMEM)
    hbm = pl.BlockSpec(memory_space=pl.ANY)

    packed = pl.pallas_call(
        functools.partial(pack_kernel, members, fold),
        out_shape=jax.ShapeDtypeStruct((members, 3, piece, part * fold), jnp.bfloat16),
        name="pack",
    )(queries, keys, values)
    packed = lax.all_to_all(packed, "vit", split_axis=0, concat_axis=0, tiled=True)

    wide = w_out.shape[0] // CHUNKS
    up_pieces, up_arrays = gather_pieces(w_in)
    down = [gather_pieces(w_out[c * wide : (c + 1) * wide]) for c in range(CHUNKS)]

    image_ids = jnp.repeat(image_of_group[0], 4)
    attended = pl.pallas_call(
        functools.partial(attend_kernel, heads, fold),
        out_shape=jax.ShapeDtypeStruct((members, piece, part * fold), jnp.bfloat16),
        scratch_shapes=[pltpu.VMEM((heads, group, LANES), jnp.bfloat16)] * 3,
        name="attend",
    )(image_ids[:, None], image_ids[None, :], packed)
    attended = lax.all_to_all(attended, "vit", split_axis=0, concat_axis=0, tiled=True)

    normed = pl.pallas_call(
        functools.partial(project_kernel, fold),
        out_shape=jax.ShapeDtypeStruct((row_count, feature_width), jnp.bfloat16),
        scratch_shapes=[pltpu.VMEM((row_count, feature_width), jnp.bfloat16)],
        name="project",
    )(attended, patch_states, out_proj, merge_gain[None, :])
    merge_rows = normed.reshape(row_count // 4, 4 * feature_width)

    half = merge_rows.shape[0] // 2
    above, below = merge_rows[:half], merge_rows[half:]
    up_blocks, down_blocks = {0: above}, {0: below}
    for step in range(1, members):
        above = ring(above, 1)
        below = ring(below, -1)
        up_blocks[members - step] = above
        down_blocks[step] = below
    row_blocks = [up_blocks[i] for i in range(members)] + [down_blocks[i] for i in range(members)]

    rows_all = row_count // 4 * members
    hid = w_in.shape[1]
    sum_shapes = [jax.ShapeDtypeStruct((half, senders * wide), jnp.bfloat16)] * (2 * members)
    results = pl.pallas_call(
        functools.partial(hidden_kernel, up_pieces, down[0][0], members),
        out_shape=[jax.ShapeDtypeStruct((rows_all, hid), jnp.bfloat16)] + sum_shapes,
        in_specs=[smem] + [vmem] * (2 * members) + [hbm] * (len(up_pieces) + len(down[0][0])),
        out_specs=[vmem] * (1 + 2 * members),
        scratch_shapes=[
            pltpu.VMEM((senders, rows_all, w_in.shape[0]), jnp.bfloat16),
            pltpu.VMEM((senders,) + w_in.shape, jnp.bfloat16),
            pltpu.VMEM((senders, wide, hid), jnp.bfloat16),
            pltpu.VMEM((rows_all, hid), jnp.float32),
            pltpu.SemaphoreType.DMA((senders,)),
            pltpu.SemaphoreType.DMA((senders,)),
        ],
        cost_estimate=pl.CostEstimate(
            flops=2 * rows_all * hid * senders * (w_in.shape[0] + wide),
            bytes_accessed=2 * hid * senders * (w_in.shape[0] + wide),
            transcendentals=0,
        ),
        name="hidden",
    )(me, *row_blocks, *up_arrays, *down[0][1])
    hidden, sums = results[0], [results[1:]]
    for c in range(1, CHUNKS):
        sums.append(
            pl.pallas_call(
                functools.partial(sums_kernel, down[c][0], members),
                out_shape=sum_shapes,
                in_specs=[smem, vmem] + [hbm] * len(down[c][0]),
                out_specs=[vmem] * (2 * members),
                scratch_shapes=[
                    pltpu.VMEM((senders, wide, hid), jnp.bfloat16),
                    pltpu.SemaphoreType.DMA((senders,)),
                ],
                cost_estimate=pl.CostEstimate(
                    flops=2 * rows_all * hid * senders * wide,
                    bytes_accessed=2 * hid * senders * wide,
                    transcendentals=0,
                ),
                name="sums",
            )(me, hidden, *down[c][1])
        )

    blocks = block_dest.shape[1]
    block_height = merge_rows.shape[0] // blocks
    destination = block_dest[0]
    positions = jnp.arange(blocks, dtype=jnp.int32)
    earlier = (destination[:, None] == destination[None, :]) & (
        positions[None, :] < positions[:, None]
    )
    slot_rank = jnp.sum(earlier.astype(jnp.int32), axis=1)
    slot_index = destination * 2 + slot_rank
    row_slots = (
        slot_index[:, None] * block_height + jnp.arange(block_height, dtype=jnp.int32)[None, :]
    ).reshape(-1)
    slots = 2 * senders * block_height
    selector = (jnp.arange(slots, dtype=jnp.int32)[:, None] == row_slots[None, :]).astype(
        jnp.bfloat16
    )
    first_row = placeholder_rows[0]
    targets = jnp.where(
        first_row[:, None] >= 0,
        first_row[:, None] + jnp.arange(block_height, dtype=jnp.int32)[None, :],
        -1,
    ).reshape(-1)
    placement = jnp.arange(text_embeds.shape[0], dtype=jnp.int32)[:, None] == targets[None, :]
    covered = jnp.any(placement, axis=1, keepdims=True).astype(jnp.int32)
    placement = placement.astype(jnp.bfloat16)

    arrived = []
    for c in range(CHUNKS):
        upper, lower = sums[c][:members], sums[c][members:]
        plus, minus = upper[members - 1], lower[1]
        for step in range(1, members):
            plus, minus = ring(plus, 1), ring(minus, -1)
            if step < members - 1:
                plus = plus.astype(jnp.float32) + upper[members - 1 - step].astype(jnp.float32)
                minus = minus.astype(jnp.float32) + lower[1 + step].astype(jnp.float32)
                plus, minus = plus.astype(jnp.bfloat16), minus.astype(jnp.bfloat16)
        outgoing = pl.pallas_call(
            route_kernel,
            out_shape=jax.ShapeDtypeStruct((slots, senders * wide), jnp.bfloat16),
            name="route",
        )(selector, plus, upper[0], minus, lower[0])
        outgoing = outgoing.reshape(senders, 2 * block_height, senders * wide)
        incoming = lax.all_to_all(outgoing, "dp", split_axis=0, concat_axis=0, tiled=True)
        arrived.append(incoming.reshape(slots, senders * wide))

    return pl.pallas_call(
        functools.partial(place_kernel, senders),
        out_shape=jax.ShapeDtypeStruct(text_embeds.shape, jnp.bfloat16),
        name="place",
    )(covered, placement, text_embeds, *arrived)


def solution(mesh):
    placed = (
        P(("dp", "vit"), None),
        P(("dp", "vit"), None),
        P(("dp", "vit"), None),
        P(("dp", "vit"), None),
        P(),
        P(),
        P("dp", None),
        P("dp", "vit"),
        P("dp", "vit"),
        P(("dp", "vit"), None),
        P(("dp", "vit"), None),
        P(("dp", "vit"), None),
    )
    return jax.shard_map(
        body, mesh=mesh, in_specs=placed, out_specs=P(("dp", "vit"), None), check_vma=False
    )
```

```python
import functools

import jax
import jax.numpy as jnp
from jax import lax
from jax.experimental import pallas as pl
from jax.experimental.pallas import tpu as pltpu
from jax.sharding import PartitionSpec as P

HEADS = 16
HEAD_DIM = 80
EPSILON = 1e-06
LANES = 128
GROUPS = 2


def fold_of(width):
    fold = 1
    while (width * fold) % LANES:
        fold *= 2
    return fold


def pack_kernel(members, groups, fold, me_ref, q_ref, k_ref, v_ref, *refs):
    outs, buf = refs[:-1], refs[-1]
    rows, width = q_ref.shape
    part, piece = width // (members * groups), rows // fold
    for at, ref in enumerate((q_ref, k_ref, v_ref)):
        for member in range(members):
            for group in range(groups):
                low = (member * groups + group) * part
                for turn in range(fold):
                    buf[member, group, at, :, turn * part : (turn + 1) * part] = ref[
                        turn * piece : (turn + 1) * piece, low : low + part
                    ]
    for group in range(groups):
        for shift in range(members):
            outs[group * members + shift][...] = buf[lax.rem(me_ref[0] + shift, members), group]


def attend_kernel(members, heads, fold, ids_col_ref, ids_row_ref, *refs):
    packed, outs, (q_buf, k_buf, v_buf) = refs[:members], refs[members:-3], refs[-3:]
    _, piece, _ = packed[0].shape
    part, rows_each = heads * HEAD_DIM, piece * fold
    lane = lax.broadcasted_iota(jnp.int32, (piece, LANES - HEAD_DIM), 1)
    ones = jnp.where(lane == 0, 1.0, 0.0).astype(jnp.bfloat16)
    zeros = jnp.zeros((piece, LANES - HEAD_DIM), jnp.bfloat16)
    for head in range(heads):
        for turn in range(fold):
            low = turn * part + head * HEAD_DIM
            for at, ref in enumerate(packed):
                rows = slice((at * fold + turn) * piece, (at * fold + turn + 1) * piece)
                q_buf[head, rows, :HEAD_DIM] = ref[0, :, low : low + HEAD_DIM]
                k_buf[head, rows, :HEAD_DIM] = ref[1, :, low : low + HEAD_DIM]
                v_buf[head, rows, :HEAD_DIM] = ref[2, :, low : low + HEAD_DIM]
                q_buf[head, rows, HEAD_DIM:] = zeros
                k_buf[head, rows, HEAD_DIM:] = zeros
                v_buf[head, rows, HEAD_DIM:] = ones
    for at, out_ref in enumerate(outs):
        rows = slice(at * rows_each, (at + 1) * rows_each)
        allowed = ids_col_ref[rows, :] == ids_row_ref[...]
        for head in range(heads):
            scores = lax.dot_general(
                q_buf[head, rows, :],
                k_buf[head],
                (((1,), (1,)), ((), ())),
                preferred_element_type=jnp.float32,
            )
            scores = jnp.where(allowed, scores, -1e30)
            highest = jnp.max(scores, axis=-1, keepdims=True)
            weights = jnp.exp((scores - highest) * HEAD_DIM ** (-0.5)).astype(jnp.bfloat16)
            mixed = jnp.dot(weights, v_buf[head], preferred_element_type=jnp.float32)
            mixed = (mixed[:, :HEAD_DIM] / mixed[:, HEAD_DIM : HEAD_DIM + 1]).astype(jnp.bfloat16)
            for turn in range(fold):
                low = turn * part + head * HEAD_DIM
                out_ref[:, low : low + HEAD_DIM] = mixed[turn * piece : (turn + 1) * piece]


def project_kernel(members, groups, fold, me_ref, patch_ref, proj_ref, gain_ref, *refs):
    packed, (above_ref, below_ref, rows_buf, normed) = refs[:-4], refs[-4:]
    piece, wide = packed[0].shape
    part = wide // fold
    depth = groups * part
    residual = patch_ref[...].astype(jnp.float32)
    for shift in range(members):
        for group in range(groups):
            for turn in range(fold):
                rows_buf[
                    shift, turn * piece : (turn + 1) * piece, group * part : (group + 1) * part
                ] = packed[group * members + shift][:, turn * part : (turn + 1) * part]
        low = pl.multiple_of(lax.rem(me_ref[0] + shift, members) * depth, depth)
        residual += jnp.dot(
            rows_buf[shift], proj_ref[pl.ds(low, depth), :], preferred_element_type=jnp.float32
        )
    mean_square = jnp.mean(residual * residual, axis=-1, keepdims=True)
    states = residual * lax.rsqrt(mean_square + EPSILON) * gain_ref[...]
    half, width = above_ref.shape[0], residual.shape[1]
    for tile in range(width // LANES):
        normed[tile] = states[:, tile * LANES : (tile + 1) * LANES]
    for at in range(4):
        for tile in range(width // LANES):
            columns = slice(at * width + tile * LANES, at * width + (tile + 1) * LANES)
            for ref, low in ((above_ref, at), (below_ref, 4 * half + at)):
                ref[:, columns] = normed[tile, pl.ds(low, half, stride=4), :].astype(jnp.bfloat16)


def hidden_kernel(pieces, more, count, me_ref, *refs):
    blocks, refs = refs[:count], refs[count:]
    first, refs = refs[: len(pieces)], refs[len(pieces) :]
    second, refs = refs[: len(more)], refs[len(more) :]
    hidden_ref, refs = refs[0], refs[1:]
    sums, refs = refs[:count], refs[count:]
    rows_buf, up_buf, down_buf, acc, up_sem, down_sem = refs
    fetch(pieces, first, up_buf, up_sem)
    fetch(more, second, down_buf, down_sem)
    members, _, depth = rows_buf.shape
    half = blocks[0].shape[0]
    for at, block in enumerate(blocks):
        for k in range(members):
            rows_buf[k, at * half : (at + 1) * half, :] = block[:, k * depth : (k + 1) * depth]
    acc[...] = jnp.zeros_like(acc)

    def one_piece(mask, carry):
        arrive(up_buf, up_sem, mask)
        acc[...] += jnp.dot(
            rows_buf[me_ref[0] ^ mask], up_buf[mask], preferred_element_type=jnp.float32
        )
        return carry

    lax.fori_loop(0, members, one_piece, 0)
    total = acc[...]
    hidden_ref[...] = (0.5 * total * (1.0 + lax.erf(total * 0.5**0.5))).astype(jnp.bfloat16)
    contract(me_ref, hidden_ref, down_buf, down_sem, sums)


def sums_kernel(pieces, count, me_ref, early_ref, late_ref, *refs):
    given, refs = refs[: len(pieces)], refs[len(pieces) :]
    sums, (hidden_buf, down_buf, down_sem) = refs[:count], refs[count:]
    fetch(pieces, given, down_buf, down_sem)
    early = early_ref.shape[0]
    hidden_buf[:early] = early_ref[...]
    hidden_buf[early:] = late_ref[...]
    contract(me_ref, hidden_buf, down_buf, down_sem, sums)


def fetch(pieces, refs, buf, sem):
    for (mask, low, length), ref in zip(pieces, refs):
        pltpu.make_async_copy(ref, buf.at[mask, pl.ds(low, length)], sem.at[mask]).start()


def arrive(buf, sem, mask):
    pltpu.make_async_copy(buf.at[mask], buf.at[mask], sem.at[mask]).wait()


def contract(me_ref, hidden_ref, down_buf, down_sem, sums):
    count, wide, _ = down_buf.shape
    half = sums[0].shape[0]

    def one_piece(mask, carry):
        arrive(down_buf, down_sem, mask)
        product = lax.dot_general(
            hidden_ref[...],
            down_buf[mask],
            (((1,), (1,)), ((), ())),
            preferred_element_type=jnp.float32,
        ).astype(jnp.bfloat16)
        low = pl.multiple_of((me_ref[0] ^ mask) * wide, wide)
        for at, ref in enumerate(sums):
            ref[:, pl.ds(low, wide)] = product[at * half : (at + 1) * half]
        return carry

    lax.fori_loop(0, count, one_piece, 0)


def route_kernel(selector_ref, plus_ref, plus_own_ref, minus_ref, minus_own_ref, *outs):
    plus = plus_ref[...].astype(jnp.float32) + plus_own_ref[...].astype(jnp.float32)
    minus = minus_ref[...].astype(jnp.float32) + minus_own_ref[...].astype(jnp.float32)
    merged = jnp.concatenate([plus.astype(jnp.bfloat16), minus.astype(jnp.bfloat16)], axis=0)
    routed = jnp.dot(selector_ref[...], merged, preferred_element_type=jnp.float32).astype(
        jnp.bfloat16
    )
    each = outs[0].shape[0]
    for at, ref in enumerate(outs):
        ref[...] = routed[at * each : (at + 1) * each]


def line_up(arrived, rows_buf):
    each = arrived[0].shape[0]
    for at, ref in enumerate(arrived):
        rows_buf[at * each : (at + 1) * each, :] = ref[...]


def place_first_kernel(covered_ref, placement_ref, text_ref, *refs):
    arrived, (out_ref, rows_buf) = refs[:-2], refs[-2:]
    line_up(arrived, rows_buf)
    wide = rows_buf.shape[1]
    placed = jnp.dot(
        placement_ref[...], rows_buf[...], preferred_element_type=jnp.float32
    ).astype(jnp.bfloat16)
    out_ref[:, :wide] = jnp.where(covered_ref[...] > 0, placed, text_ref[:, :wide])
    out_ref[:, wide:] = text_ref[:, wide:]


def place_last_kernel(step, covered_ref, placement_ref, given_ref, *refs):
    arrived, (out_ref, rows_buf, before, result, in_sem, out_sem) = refs[:-6], refs[-6:]
    count, _, wide = before.shape

    def window(ref, at):
        return ref.at[:, pl.ds(at * step + step - wide, wide)]

    reads = [
        pltpu.make_async_copy(window(given_ref, at), before.at[at], in_sem.at[at])
        for at in range(count)
    ]
    writes = [
        pltpu.make_async_copy(result.at[at], window(out_ref, at), out_sem.at[at])
        for at in range(count)
    ]
    for read in reads:
        read.start()
    line_up(arrived, rows_buf)
    covered = covered_ref[...] > 0
    for at in range(count):
        placed = jnp.dot(
            placement_ref[...],
            rows_buf[:, at * wide : (at + 1) * wide],
            preferred_element_type=jnp.float32,
        ).astype(jnp.bfloat16)
        reads[at].wait()
        result[at] = jnp.where(covered, placed, before[at])
        writes[at].start()
    for write in writes:
        write.wait()


def ring(value, step):
    members = lax.axis_size("vit")
    return lax.ppermute(value, "vit", [(i, (i + step) % members) for i in range(members)])


def gather_pieces(value):
    senders, rows = lax.axis_size("dp"), value.shape[0]
    side = 1
    while 2 * side * side < senders:
        side *= 2
    along_x, along_y = 2 * (side - 1), 2 * side * (side - 1)
    unit = 128 if rows >= 256 else 16
    cut = rows // 2 // unit * unit

    def swap(part, bit):
        low, array = part
        return low, lax.ppermute(array, "dp", [(i, i ^ bit) for i in range(senders)])

    def part_of(parts, top):
        if len(parts) == 2:
            return parts[0 if top else 1]
        array = parts[0][1]
        return (0, array[:cut]) if top else (cut, array[cut:])

    def high(mask):
        return 1 << (mask.bit_length() - 1)

    found = {0: [(0, value)]}
    for mask in range(2, senders, 2):
        x, y = mask & along_x, mask & along_y
        if x and y:
            top = part_of(found[x | (y ^ high(y))], True)
            bottom = part_of(found[(x ^ high(x)) | y], False)
            found[mask] = [swap(top, high(y)), swap(bottom, high(x))]
        else:
            found[mask] = [swap(p, high(mask)) for p in found[mask ^ high(mask)]]
    for mask in range(1, senders, 2):
        found[mask] = [swap(p, 1) for p in found[mask ^ 1]]
    order = [(mask, low, a) for mask in range(senders) for low, a in found[mask]]
    return [(mask, low, a.shape[0]) for mask, low, a in order], [a for _, _, a in order]


def kernel(body, **options):
    return pl.pallas_call(body, **options)


def body(
    patch_states,
    queries,
    keys,
    values,
    out_proj,
    merge_gain,
    image_of_group,
    w_in,
    w_out,
    text_embeds,
    block_dest,
    placeholder_rows,
):
    row_count, feature_width = queries.shape
    members = lax.axis_size("vit")
    senders = lax.axis_size("dp")
    me = lax.axis_index("dp").astype(jnp.int32)[None]
    member = lax.axis_index("vit").astype(jnp.int32)
    heads = HEADS // members // GROUPS
    fold = fold_of(heads * HEAD_DIM)
    piece, packed_width = row_count // fold, heads * HEAD_DIM * fold
    vmem = pl.BlockSpec(memory_space=pltpu.VMEM)
    smem = pl.BlockSpec(memory_space=pltpu.SMEM)
    hbm = pl.BlockSpec(memory_space=pl.ANY)

    packed = kernel(
functools.partial(pack_kernel, members, GROUPS, fold),
        out_shape=[jax.ShapeDtypeStruct((3, piece, packed_width), jnp.bfloat16)]
        * (GROUPS * members),
        in_specs=[smem] + [vmem] * 3,
        out_specs=[vmem] * (GROUPS * members),
        scratch_shapes=[pltpu.VMEM((members, GROUPS, 3, piece, packed_width), jnp.bfloat16)],
    )(member[None], queries, keys, values)
    arrived = [
        [
            packed[g * members + s]
            if s == 0
            else ring(packed[g * members + s], s)
            for s in range(members)
        ]
        for g in range(GROUPS)
    ]

    image_ids = jnp.repeat(image_of_group[0], 4)
    shifts = lax.rem(member + members - jnp.arange(members, dtype=jnp.int32), members)
    image_ids = image_ids.reshape(members, row_count)[shifts].reshape(-1)
    returned = []
    for g in range(GROUPS):
        attended = kernel(
functools.partial(attend_kernel, members, heads, fold),
            out_shape=[jax.ShapeDtypeStruct((piece, packed_width), jnp.bfloat16)] * members,
            in_specs=[vmem] * (2 + members),
            out_specs=[vmem] * members,
            scratch_shapes=[pltpu.VMEM((heads, row_count * members, LANES), jnp.bfloat16)] * 3,
            cost_estimate=pl.CostEstimate(
                flops=8 * heads * LANES * (row_count * members) ** 2,
                bytes_accessed=8 * row_count * feature_width,
                transcendentals=heads * (row_count * members) ** 2,
            ),
        )(image_ids[:, None], image_ids[None, :], *arrived[g])
        returned += [attended[s] if s == 0 else ring(attended[s], -s) for s in range(members)]

    half, merge_width = row_count // 8, 4 * feature_width
    above, below = kernel(
        functools.partial(project_kernel, members, GROUPS, fold),
        out_shape=[jax.ShapeDtypeStruct((half, merge_width), jnp.bfloat16)] * 2,
        in_specs=[smem] + [vmem] * (3 + GROUPS * members),
        out_specs=[vmem] * 2,
        scratch_shapes=[
            pltpu.VMEM((members, row_count, feature_width // members), jnp.bfloat16),
            pltpu.VMEM((feature_width // LANES, row_count, LANES), jnp.float32),
        ],
    )(member[None], patch_states, out_proj, merge_gain[None, :], *returned)

    rows = {("up", 0): above, ("low", 0): below}
    for step in range(1, members):
        above = ring(above, 1)
        below = ring(below, -1)
        rows["up", members - step] = above
        rows["low", step] = below
    late = [("up", 1), ("low", members - 1)]
    early = [name for name in rows if name not in late]

    units = w_out.shape[0] // LANES
    widths = [(units - max(1, units * 3 // 8)) * LANES, max(1, units * 3 // 8) * LANES]
    up_pieces, up_arrays = gather_pieces(w_in)
    down = [gather_pieces(w_out[: widths[0]]), gather_pieces(w_out[widths[0] :])]
    hid = w_in.shape[1]

    def weight_cost(count, *parts):
        size = hid * senders * sum(parts)
        return pl.CostEstimate(flops=2 * count * size, bytes_accessed=2 * size, transcendentals=0)

    def sum_shape(chunk):
        return jax.ShapeDtypeStruct((half, senders * widths[chunk]), jnp.bfloat16)

    hidden, sums = [], [{}, {}]
    for names in (early, late):
        count = len(names)
        results = kernel(
            functools.partial(hidden_kernel, up_pieces, down[0][0], count),
            out_shape=[jax.ShapeDtypeStruct((count * half, hid), jnp.bfloat16)]
            + [sum_shape(0)] * count,
            in_specs=[smem] + [vmem] * count + [hbm] * (len(up_pieces) + len(down[0][0])),
            out_specs=[vmem] * (1 + count),
            scratch_shapes=[
                pltpu.VMEM((senders, count * half, w_in.shape[0]), jnp.bfloat16),
                pltpu.VMEM((senders,) + w_in.shape, jnp.bfloat16),
                pltpu.VMEM((senders, widths[0], hid), jnp.bfloat16),
                pltpu.VMEM((count * half, hid), jnp.float32),
                pltpu.SemaphoreType.DMA((senders,)),
                pltpu.SemaphoreType.DMA((senders,)),
            ],
            cost_estimate=weight_cost(count * half, w_in.shape[0], widths[0]),
        )(me, *[rows[name] for name in names], *up_arrays, *down[0][1])
        hidden.append(results[0])
        sums[0].update(zip(names, results[1:]))
    count = 2 * members
    results = kernel(
        functools.partial(sums_kernel, down[1][0], count),
        out_shape=[sum_shape(1)] * count,
        in_specs=[smem, vmem, vmem] + [hbm] * len(down[1][0]),
        out_specs=[vmem] * count,
        scratch_shapes=[
            pltpu.VMEM((count * half, hid), jnp.bfloat16),
            pltpu.VMEM((senders, widths[1], hid), jnp.bfloat16),
            pltpu.SemaphoreType.DMA((senders,)),
        ],
        cost_estimate=weight_cost(count * half, widths[1]),
    )(me, *hidden, *down[1][1])
    sums[1].update(zip(early + late, results))

    blocks = block_dest.shape[1]
    block_height = 2 * half // blocks
    slots, text_rows = 2 * senders * block_height, text_embeds.shape[0]
    height = jnp.arange(block_height, dtype=jnp.int32)[None, :]
    destination = block_dest[0]
    positions = jnp.arange(blocks, dtype=jnp.int32)
    earlier = (destination[:, None] == destination[None, :]) & (
        positions[None, :] < positions[:, None]
    )
    slot_rank = jnp.sum(earlier.astype(jnp.int32), axis=1)
    slot_index = (destination ^ me) * 2 + slot_rank
    row_slots = (slot_index[:, None] * block_height + height).reshape(-1)
    selector = (jnp.arange(slots, dtype=jnp.int32)[:, None] == row_slots[None, :]).astype(
        jnp.bfloat16
    )
    others = jnp.arange(senders, dtype=jnp.int32) ^ me
    first_row = placeholder_rows.reshape(senders, 2)[others].reshape(-1)
    targets = jnp.where(first_row[:, None] >= 0, first_row[:, None] + height, -1).reshape(-1)
    placement = jnp.arange(text_rows, dtype=jnp.int32)[:, None] == targets[None, :]
    covered = jnp.any(placement, axis=1, keepdims=True).astype(jnp.int32)
    placement = placement.astype(jnp.bfloat16)

    text, step_width = text_embeds, w_out.shape[0]
    for c, wide in enumerate(widths):
        width = senders * wide
        plus, minus = sums[c]["up", members - 1], sums[c]["low", 1]
        for step in range(1, members):
            if step > 1:
                plus = plus.astype(jnp.float32) + sums[c]["up", members - step].astype(jnp.float32)
                minus = minus.astype(jnp.float32) + sums[c]["low", step].astype(jnp.float32)
            plus = ring(plus.astype(jnp.bfloat16), 1)
            minus = ring(minus.astype(jnp.bfloat16), -1)
        each = 2 * block_height
        routed = kernel(
            route_kernel,
            out_shape=[jax.ShapeDtypeStruct((each, width), jnp.bfloat16)] * senders,
            in_specs=[vmem] * 5,
            out_specs=[vmem] * senders,
        )(selector, plus, sums[c]["up", 0], minus, sums[c]["low", 0])
        incoming = [routed[0]]
        for mask in range(1, senders):
            incoming.append(
                lax.ppermute(routed[mask], "dp", [(i, i ^ mask) for i in range(senders)])
            )
        if c == 0:
            columns = pl.BlockSpec((text_rows, step_width), lambda at: (0, at))
            text = kernel(
                place_first_kernel,
                grid=(senders,),
                out_shape=jax.ShapeDtypeStruct(text_embeds.shape, jnp.bfloat16),
                in_specs=[
                    pl.BlockSpec((text_rows, 1), lambda at: (0, 0)),
                    pl.BlockSpec((text_rows, slots), lambda at: (0, 0)),
                    columns,
                ]
                + [pl.BlockSpec((each, wide), lambda at: (0, at))] * senders,
                out_specs=columns,
                scratch_shapes=[pltpu.VMEM((slots, wide), jnp.bfloat16)],
            )(covered, placement, text_embeds, *incoming)
        else:
            text = kernel(
                functools.partial(place_last_kernel, step_width),
                out_shape=jax.ShapeDtypeStruct(text_embeds.shape, jnp.bfloat16),
                in_specs=[vmem, vmem, hbm] + [vmem] * senders,
                out_specs=hbm,
                scratch_shapes=[
                    pltpu.VMEM((slots, width), jnp.bfloat16),
                    pltpu.VMEM((senders, text_rows, wide), jnp.bfloat16),
                    pltpu.VMEM((senders, text_rows, wide), jnp.bfloat16),
                    pltpu.SemaphoreType.DMA((senders,)),
                    pltpu.SemaphoreType.DMA((senders,)),
                ],
                input_output_aliases={2: 0},
            )(covered, placement, text, *incoming)
    return text


def solution(mesh):
    placed = (
        P(("dp", "vit"), None),
        P(("dp", "vit"), None),
        P(("dp", "vit"), None),
        P(("dp", "vit"), None),
        P(),
        P(),
        P("dp", None),
        P("dp", "vit"),
        P("dp", "vit"),
        P(("dp", "vit"), None),
        P(("dp", "vit"), None),
        P(("dp", "vit"), None),
    )

    return jax.shard_map(
        body, mesh=mesh, in_specs=placed, out_specs=P(("dp", "vit"), None), check_vma=False
    )
```

```python
import functools

import jax
import jax.numpy as jnp
from jax import lax
from jax.experimental import pallas as pl
from jax.experimental.pallas import tpu as pltpu
from jax.sharding import PartitionSpec as P

HEADS = 16
HEAD_DIM = 80
EPSILON = 1e-06
LANES = 128
GROUPS = 2


def fold_of(width):
    fold = 1
    while (width * fold) % LANES:
        fold *= 2
    return fold


def pack_kernel(members, groups, fold, me_ref, q_ref, k_ref, v_ref, *refs):
    outs, buf = refs[:-1], refs[-1]
    rows, width = q_ref.shape
    part, piece = width // (members * groups), rows // fold
    for at, ref in enumerate((q_ref, k_ref, v_ref)):
        for member in range(members):
            for group in range(groups):
                low = (member * groups + group) * part
                for turn in range(fold):
                    buf[member, group, at, :, turn * part : (turn + 1) * part] = ref[
                        turn * piece : (turn + 1) * piece, low : low + part
                    ]
    for group in range(groups):
        for shift in range(members):
            outs[group * members + shift][...] = buf[lax.rem(me_ref[0] + shift, members), group]


def attend_kernel(members, heads, fold, ids_col_ref, ids_row_ref, *refs):
    packed, outs, (q_buf, k_buf, v_buf) = refs[:members], refs[members:-3], refs[-3:]
    _, piece, _ = packed[0].shape
    part, rows_each = heads * HEAD_DIM, piece * fold
    lane = lax.broadcasted_iota(jnp.int32, (piece, LANES - HEAD_DIM), 1)
    ones = jnp.where(lane == 0, 1.0, 0.0).astype(jnp.bfloat16)
    zeros = jnp.zeros((piece, LANES - HEAD_DIM), jnp.bfloat16)
    for head in range(heads):
        for turn in range(fold):
            low = turn * part + head * HEAD_DIM
            for at, ref in enumerate(packed):
                rows = slice((at * fold + turn) * piece, (at * fold + turn + 1) * piece)
                q_buf[head, rows, :HEAD_DIM] = ref[0, :, low : low + HEAD_DIM]
                k_buf[head, rows, :HEAD_DIM] = ref[1, :, low : low + HEAD_DIM]
                v_buf[head, rows, :HEAD_DIM] = ref[2, :, low : low + HEAD_DIM]
                q_buf[head, rows, HEAD_DIM:] = zeros
                k_buf[head, rows, HEAD_DIM:] = zeros
                v_buf[head, rows, HEAD_DIM:] = ones
    for at, out_ref in enumerate(outs):
        rows = slice(at * rows_each, (at + 1) * rows_each)
        allowed = ids_col_ref[rows, :] == ids_row_ref[...]
        for head in range(heads):
            scores = lax.dot_general(
                q_buf[head, rows, :],
                k_buf[head],
                (((1,), (1,)), ((), ())),
                preferred_element_type=jnp.float32,
            )
            scores = jnp.where(allowed, scores, -1e30)
            highest = jnp.max(scores, axis=-1, keepdims=True)
            weights = jnp.exp((scores - highest) * HEAD_DIM ** (-0.5)).astype(jnp.bfloat16)
            mixed = jnp.dot(weights, v_buf[head], preferred_element_type=jnp.float32)
            mixed = (mixed[:, :HEAD_DIM] / mixed[:, HEAD_DIM : HEAD_DIM + 1]).astype(jnp.bfloat16)
            for turn in range(fold):
                low = turn * part + head * HEAD_DIM
                out_ref[:, low : low + HEAD_DIM] = mixed[turn * piece : (turn + 1) * piece]


def project_kernel(members, groups, fold, me_ref, patch_ref, proj_ref, gain_ref, *refs):
    packed, (above_ref, below_ref, rows_buf, normed) = refs[:-4], refs[-4:]
    piece, wide = packed[0].shape
    part = wide // fold
    depth = groups * part
    residual = patch_ref[...].astype(jnp.float32)
    for shift in range(members):
        for group in range(groups):
            for turn in range(fold):
                rows_buf[
                    shift, turn * piece : (turn + 1) * piece, group * part : (group + 1) * part
                ] = packed[group * members + shift][:, turn * part : (turn + 1) * part]
        low = pl.multiple_of(lax.rem(me_ref[0] + shift, members) * depth, depth)
        residual += jnp.dot(
            rows_buf[shift], proj_ref[pl.ds(low, depth), :], preferred_element_type=jnp.float32
        )
    mean_square = jnp.mean(residual * residual, axis=-1, keepdims=True)
    states = residual * lax.rsqrt(mean_square + EPSILON) * gain_ref[...]
    half, width = above_ref.shape[0], residual.shape[1]
    for tile in range(width // LANES):
        normed[tile] = states[:, tile * LANES : (tile + 1) * LANES]
    for at in range(4):
        for tile in range(width // LANES):
            columns = slice(at * width + tile * LANES, at * width + (tile + 1) * LANES)
            for ref, low in ((above_ref, at), (below_ref, 4 * half + at)):
                ref[:, columns] = normed[tile, pl.ds(low, half, stride=4), :].astype(jnp.bfloat16)


def hidden_kernel(pieces, more, count, me_ref, *refs):
    blocks, refs = refs[:count], refs[count:]
    first, refs = refs[: len(pieces)], refs[len(pieces) :]
    second, refs = refs[: len(more)], refs[len(more) :]
    hidden_ref, refs = refs[0], refs[1:]
    sums, refs = refs[:count], refs[count:]
    rows_buf, up_buf, down_buf, acc, up_sem, down_sem = refs
    fetch(pieces, first, up_buf, up_sem)
    fetch(more, second, down_buf, down_sem)
    members, _, depth = rows_buf.shape
    half = blocks[0].shape[0]
    for at, block in enumerate(blocks):
        for k in range(members):
            rows_buf[k, at * half : (at + 1) * half, :] = block[:, k * depth : (k + 1) * depth]
    acc[...] = jnp.zeros_like(acc)

    def one_piece(mask, carry):
        arrive(up_buf, up_sem, mask)
        acc[...] += jnp.dot(
            rows_buf[me_ref[0] ^ mask], up_buf[mask], preferred_element_type=jnp.float32
        )
        return carry

    lax.fori_loop(0, members, one_piece, 0)
    total = acc[...]
    hidden_ref[...] = (0.5 * total * (1.0 + lax.erf(total * 0.5**0.5))).astype(jnp.bfloat16)
    contract(me_ref, hidden_ref, down_buf, down_sem, sums)


def sums_kernel(pieces, count, me_ref, early_ref, late_ref, *refs):
    given, refs = refs[: len(pieces)], refs[len(pieces) :]
    sums, (hidden_buf, down_buf, down_sem) = refs[:count], refs[count:]
    fetch(pieces, given, down_buf, down_sem)
    early = early_ref.shape[0]
    hidden_buf[:early] = early_ref[...]
    hidden_buf[early:] = late_ref[...]
    contract(me_ref, hidden_buf, down_buf, down_sem, sums)


def fetch(pieces, refs, buf, sem):
    for (mask, low, length), ref in zip(pieces, refs):
        pltpu.make_async_copy(ref, buf.at[mask, pl.ds(low, length)], sem.at[mask]).start()


def arrive(buf, sem, mask):
    pltpu.make_async_copy(buf.at[mask], buf.at[mask], sem.at[mask]).wait()


def contract(me_ref, hidden_ref, down_buf, down_sem, sums):
    count, wide, _ = down_buf.shape
    half = sums[0].shape[0]

    def one_piece(mask, carry):
        arrive(down_buf, down_sem, mask)
        product = lax.dot_general(
            hidden_ref[...],
            down_buf[mask],
            (((1,), (1,)), ((), ())),
            preferred_element_type=jnp.float32,
        ).astype(jnp.bfloat16)
        low = pl.multiple_of((me_ref[0] ^ mask) * wide, wide)
        for at, ref in enumerate(sums):
            ref[:, pl.ds(low, wide)] = product[at * half : (at + 1) * half]
        return carry

    lax.fori_loop(0, count, one_piece, 0)


def route_kernel(selector_ref, plus_ref, plus_own_ref, minus_ref, minus_own_ref, *outs):
    plus = plus_ref[...].astype(jnp.float32) + plus_own_ref[...].astype(jnp.float32)
    minus = minus_ref[...].astype(jnp.float32) + minus_own_ref[...].astype(jnp.float32)
    merged = jnp.concatenate([plus.astype(jnp.bfloat16), minus.astype(jnp.bfloat16)], axis=0)
    routed = jnp.dot(selector_ref[...], merged, preferred_element_type=jnp.float32).astype(
        jnp.bfloat16
    )
    each = outs[0].shape[0]
    for at, ref in enumerate(outs):
        ref[...] = routed[at * each : (at + 1) * each]


def line_up(arrived, rows_buf):
    each = arrived[0].shape[0]
    for at, ref in enumerate(arrived):
        rows_buf[at * each : (at + 1) * each, :] = ref[...]


def place_first_kernel(covered_ref, placement_ref, text_ref, *refs):
    arrived, (out_ref, rows_buf) = refs[:-2], refs[-2:]
    line_up(arrived, rows_buf)
    wide = rows_buf.shape[1]
    placed = jnp.dot(
        placement_ref[...], rows_buf[...], preferred_element_type=jnp.float32
    ).astype(jnp.bfloat16)
    out_ref[:, :wide] = jnp.where(covered_ref[...] > 0, placed, text_ref[:, :wide])
    out_ref[:, wide:] = text_ref[:, wide:]


def place_last_kernel(step, covered_ref, placement_ref, given_ref, *refs):
    arrived, (out_ref, rows_buf, before, result, in_sem, out_sem) = refs[:-6], refs[-6:]
    count, _, wide = before.shape

    def window(ref, at):
        return ref.at[:, pl.ds(at * step + step - wide, wide)]

    reads = [
        pltpu.make_async_copy(window(given_ref, at), before.at[at], in_sem.at[at])
        for at in range(count)
    ]
    writes = [
        pltpu.make_async_copy(result.at[at], window(out_ref, at), out_sem.at[at])
        for at in range(count)
    ]
    for read in reads:
        read.start()
    line_up(arrived, rows_buf)
    covered = covered_ref[...] > 0
    for at in range(count):
        placed = jnp.dot(
            placement_ref[...],
            rows_buf[:, at * wide : (at + 1) * wide],
            preferred_element_type=jnp.float32,
        ).astype(jnp.bfloat16)
        reads[at].wait()
        result[at] = jnp.where(covered, placed, before[at])
        writes[at].start()
    for write in writes:
        write.wait()


def ring(value, step):
    members = lax.axis_size("vit")
    return lax.ppermute(value, "vit", [(i, (i + step) % members) for i in range(members)])


def gather_pieces(value, direct=False):
    senders, rows = lax.axis_size("dp"), value.shape[0]
    side = 1
    while 2 * side * side < senders:
        side *= 2
    along_x, along_y = 2 * (side - 1), 2 * side * (side - 1)
    unit = 128 if rows >= 256 else 16
    cut = rows // 2 // unit * unit

    def swap(part, bit):
        low, array = part
        return low, lax.ppermute(array, "dp", [(i, i ^ bit) for i in range(senders)])

    def part_of(parts, top):
        if len(parts) == 2:
            return parts[0 if top else 1]
        array = parts[0][1]
        return (0, array[:cut]) if top else (cut, array[cut:])

    def high(mask):
        return 1 << (mask.bit_length() - 1)

    found = {0: [(0, value)]}
    for mask in range(2, senders, 2):
        x, y = mask & along_x, mask & along_y
        if x and y and direct:
            found[mask] = [swap(found[0][0], mask)]
        elif x and y:
            top = part_of(found[x | (y ^ high(y))], True)
            bottom = part_of(found[(x ^ high(x)) | y], False)
            found[mask] = [swap(top, high(y)), swap(bottom, high(x))]
        else:
            found[mask] = [swap(p, high(mask)) for p in found[mask ^ high(mask)]]
    for mask in range(1, senders, 2):
        found[mask] = [swap(p, 1) for p in found[mask ^ 1]]
    order = [(mask, low, a) for mask in range(senders) for low, a in found[mask]]
    return [(mask, low, a.shape[0]) for mask, low, a in order], [a for _, _, a in order]


def kernel(body, **options):
    return pl.pallas_call(body, **options)


def body(
    patch_states,
    queries,
    keys,
    values,
    out_proj,
    merge_gain,
    image_of_group,
    w_in,
    w_out,
    text_embeds,
    block_dest,
    placeholder_rows,
):
    row_count, feature_width = queries.shape
    members = lax.axis_size("vit")
    senders = lax.axis_size("dp")
    me = lax.axis_index("dp").astype(jnp.int32)[None]
    member = lax.axis_index("vit").astype(jnp.int32)
    heads = HEADS // members // GROUPS
    fold = fold_of(heads * HEAD_DIM)
    piece, packed_width = row_count // fold, heads * HEAD_DIM * fold
    vmem = pl.BlockSpec(memory_space=pltpu.VMEM)
    smem = pl.BlockSpec(memory_space=pltpu.SMEM)
    hbm = pl.BlockSpec(memory_space=pl.ANY)

    packed = kernel(
functools.partial(pack_kernel, members, GROUPS, fold),
        out_shape=[jax.ShapeDtypeStruct((3, piece, packed_width), jnp.bfloat16)]
        * (GROUPS * members),
        in_specs=[smem] + [vmem] * 3,
        out_specs=[vmem] * (GROUPS * members),
        scratch_shapes=[pltpu.VMEM((members, GROUPS, 3, piece, packed_width), jnp.bfloat16)],
    )(member[None], queries, keys, values)
    arrived = [
        [
            packed[g * members + s]
            if s == 0
            else ring(packed[g * members + s], s)
            for s in range(members)
        ]
        for g in range(GROUPS)
    ]

    image_ids = jnp.repeat(image_of_group[0], 4)
    shifts = lax.rem(member + members - jnp.arange(members, dtype=jnp.int32), members)
    image_ids = image_ids.reshape(members, row_count)[shifts].reshape(-1)
    returned = []
    for g in range(GROUPS):
        attended = kernel(
functools.partial(attend_kernel, members, heads, fold),
            out_shape=[jax.ShapeDtypeStruct((piece, packed_width), jnp.bfloat16)] * members,
            in_specs=[vmem] * (2 + members),
            out_specs=[vmem] * members,
            scratch_shapes=[pltpu.VMEM((heads, row_count * members, LANES), jnp.bfloat16)] * 3,
            cost_estimate=pl.CostEstimate(
                flops=8 * heads * LANES * (row_count * members) ** 2,
                bytes_accessed=8 * row_count * feature_width,
                transcendentals=heads * (row_count * members) ** 2,
            ),
        )(image_ids[:, None], image_ids[None, :], *arrived[g])
        returned += [attended[s] if s == 0 else ring(attended[s], -s) for s in range(members)]

    half, merge_width = row_count // 8, 4 * feature_width
    above, below = kernel(
        functools.partial(project_kernel, members, GROUPS, fold),
        out_shape=[jax.ShapeDtypeStruct((half, merge_width), jnp.bfloat16)] * 2,
        in_specs=[smem] + [vmem] * (3 + GROUPS * members),
        out_specs=[vmem] * 2,
        scratch_shapes=[
            pltpu.VMEM((members, row_count, feature_width // members), jnp.bfloat16),
            pltpu.VMEM((feature_width // LANES, row_count, LANES), jnp.float32),
        ],
    )(member[None], patch_states, out_proj, merge_gain[None, :], *returned)

    rows = {("up", 0): above, ("low", 0): below}
    for step in range(1, members):
        above = ring(above, 1)
        below = ring(below, -1)
        rows["up", members - step] = above
        rows["low", step] = below
    late = [("up", 1), ("low", members - 1)]
    early = [name for name in rows if name not in late]

    units = w_out.shape[0] // LANES
    widths = [(units - max(1, units * 3 // 8)) * LANES, max(1, units * 3 // 8) * LANES]
    up_pieces, up_arrays = gather_pieces(w_in)
    down = [gather_pieces(w_out[: widths[0]]), gather_pieces(w_out[widths[0] :], direct=True)]
    hid = w_in.shape[1]

    def weight_cost(count, *parts):
        size = hid * senders * sum(parts)
        return pl.CostEstimate(flops=2 * count * size, bytes_accessed=2 * size, transcendentals=0)

    def sum_shape(chunk):
        return jax.ShapeDtypeStruct((half, senders * widths[chunk]), jnp.bfloat16)

    hidden, sums = [], [{}, {}]
    for names in (early, late):
        count = len(names)
        results = kernel(
            functools.partial(hidden_kernel, up_pieces, down[0][0], count),
            out_shape=[jax.ShapeDtypeStruct((count * half, hid), jnp.bfloat16)]
            + [sum_shape(0)] * count,
            in_specs=[smem] + [vmem] * count + [hbm] * (len(up_pieces) + len(down[0][0])),
            out_specs=[vmem] * (1 + count),
            scratch_shapes=[
                pltpu.VMEM((senders, count * half, w_in.shape[0]), jnp.bfloat16),
                pltpu.VMEM((senders,) + w_in.shape, jnp.bfloat16),
                pltpu.VMEM((senders, widths[0], hid), jnp.bfloat16),
                pltpu.VMEM((count * half, hid), jnp.float32),
                pltpu.SemaphoreType.DMA((senders,)),
                pltpu.SemaphoreType.DMA((senders,)),
            ],
            cost_estimate=weight_cost(count * half, w_in.shape[0], widths[0]),
        )(me, *[rows[name] for name in names], *up_arrays, *down[0][1])
        hidden.append(results[0])
        sums[0].update(zip(names, results[1:]))
    count = 2 * members
    results = kernel(
        functools.partial(sums_kernel, down[1][0], count),
        out_shape=[sum_shape(1)] * count,
        in_specs=[smem, vmem, vmem] + [hbm] * len(down[1][0]),
        out_specs=[vmem] * count,
        scratch_shapes=[
            pltpu.VMEM((count * half, hid), jnp.bfloat16),
            pltpu.VMEM((senders, widths[1], hid), jnp.bfloat16),
            pltpu.SemaphoreType.DMA((senders,)),
        ],
        cost_estimate=weight_cost(count * half, widths[1]),
    )(me, *hidden, *down[1][1])
    sums[1].update(zip(early + late, results))

    blocks = block_dest.shape[1]
    block_height = 2 * half // blocks
    slots, text_rows = 2 * senders * block_height, text_embeds.shape[0]
    height = jnp.arange(block_height, dtype=jnp.int32)[None, :]
    destination = block_dest[0]
    positions = jnp.arange(blocks, dtype=jnp.int32)
    earlier = (destination[:, None] == destination[None, :]) & (
        positions[None, :] < positions[:, None]
    )
    slot_rank = jnp.sum(earlier.astype(jnp.int32), axis=1)
    slot_index = (destination ^ me) * 2 + slot_rank
    row_slots = (slot_index[:, None] * block_height + height).reshape(-1)
    selector = (jnp.arange(slots, dtype=jnp.int32)[:, None] == row_slots[None, :]).astype(
        jnp.bfloat16
    )
    others = jnp.arange(senders, dtype=jnp.int32) ^ me
    first_row = placeholder_rows.reshape(senders, 2)[others].reshape(-1)
    targets = jnp.where(first_row[:, None] >= 0, first_row[:, None] + height, -1).reshape(-1)
    placement = jnp.arange(text_rows, dtype=jnp.int32)[:, None] == targets[None, :]
    covered = jnp.any(placement, axis=1, keepdims=True).astype(jnp.int32)
    placement = placement.astype(jnp.bfloat16)

    text, step_width = text_embeds, w_out.shape[0]
    for c, wide in enumerate(widths):
        width = senders * wide
        plus, minus = sums[c]["up", members - 1], sums[c]["low", 1]
        for step in range(1, members):
            if step > 1:
                plus = plus.astype(jnp.float32) + sums[c]["up", members - step].astype(jnp.float32)
                minus = minus.astype(jnp.float32) + sums[c]["low", step].astype(jnp.float32)
            plus = ring(plus.astype(jnp.bfloat16), 1)
            minus = ring(minus.astype(jnp.bfloat16), -1)
        each = 2 * block_height
        routed = kernel(
            route_kernel,
            out_shape=[jax.ShapeDtypeStruct((each, width), jnp.bfloat16)] * senders,
            in_specs=[vmem] * 5,
            out_specs=[vmem] * senders,
        )(selector, plus, sums[c]["up", 0], minus, sums[c]["low", 0])
        incoming = [routed[0]]
        for mask in range(1, senders):
            incoming.append(
                lax.ppermute(routed[mask], "dp", [(i, i ^ mask) for i in range(senders)])
            )
        if c == 0:
            columns = pl.BlockSpec((text_rows, step_width), lambda at: (0, at))
            text = kernel(
                place_first_kernel,
                grid=(senders,),
                out_shape=jax.ShapeDtypeStruct(text_embeds.shape, jnp.bfloat16),
                in_specs=[
                    pl.BlockSpec((text_rows, 1), lambda at: (0, 0)),
                    pl.BlockSpec((text_rows, slots), lambda at: (0, 0)),
                    columns,
                ]
                + [pl.BlockSpec((each, wide), lambda at: (0, at))] * senders,
                out_specs=columns,
                scratch_shapes=[pltpu.VMEM((slots, wide), jnp.bfloat16)],
            )(covered, placement, text_embeds, *incoming)
        else:
            text = kernel(
                functools.partial(place_last_kernel, step_width),
                out_shape=jax.ShapeDtypeStruct(text_embeds.shape, jnp.bfloat16),
                in_specs=[vmem, vmem, hbm] + [vmem] * senders,
                out_specs=hbm,
                scratch_shapes=[
                    pltpu.VMEM((slots, width), jnp.bfloat16),
                    pltpu.VMEM((senders, text_rows, wide), jnp.bfloat16),
                    pltpu.VMEM((senders, text_rows, wide), jnp.bfloat16),
                    pltpu.SemaphoreType.DMA((senders,)),
                    pltpu.SemaphoreType.DMA((senders,)),
                ],
                input_output_aliases={2: 0},
            )(covered, placement, text, *incoming)
    return text


def solution(mesh):
    placed = (
        P(("dp", "vit"), None),
        P(("dp", "vit"), None),
        P(("dp", "vit"), None),
        P(("dp", "vit"), None),
        P(),
        P(),
        P("dp", None),
        P("dp", "vit"),
        P("dp", "vit"),
        P(("dp", "vit"), None),
        P(("dp", "vit"), None),
        P(("dp", "vit"), None),
    )

    return jax.shard_map(
        body, mesh=mesh, in_specs=placed, out_specs=P(("dp", "vit"), None), check_vma=False
    )
```

```python
import functools

import jax
import jax.numpy as jnp
from jax import lax
from jax.experimental import pallas as pl
from jax.experimental.pallas import tpu as pltpu
from jax.sharding import PartitionSpec as P

HEADS = 16
HEAD_DIM = 80
EPSILON = 1e-06
LANES = 128
GROUPS = 2


def fold_of(width):
    fold = 1
    while (width * fold) % LANES:
        fold *= 2
    return fold


def pack_kernel(members, groups, fold, me_ref, q_ref, k_ref, v_ref, *refs):
    outs, buf = refs[:-1], refs[-1]
    rows, width = q_ref.shape
    part, piece = width // (members * groups), rows // fold
    for at, ref in enumerate((q_ref, k_ref, v_ref)):
        for member in range(members):
            for group in range(groups):
                low = (member * groups + group) * part
                for turn in range(fold):
                    buf[member, group, at, :, turn * part : (turn + 1) * part] = ref[
                        turn * piece : (turn + 1) * piece, low : low + part
                    ]
    for group in range(groups):
        for shift in range(members):
            outs[group * members + shift][...] = buf[lax.rem(me_ref[0] + shift, members), group]


def attend_kernel(members, heads, fold, ids_col_ref, ids_row_ref, *refs):
    packed, outs, (q_buf, k_buf, v_buf) = refs[:members], refs[members:-3], refs[-3:]
    _, piece, _ = packed[0].shape
    part, rows_each = heads * HEAD_DIM, piece * fold
    lane = lax.broadcasted_iota(jnp.int32, (piece, LANES - HEAD_DIM), 1)
    ones = jnp.where(lane == 0, 1.0, 0.0).astype(jnp.bfloat16)
    zeros = jnp.zeros((piece, LANES - HEAD_DIM), jnp.bfloat16)
    for head in range(heads):
        for turn in range(fold):
            low = turn * part + head * HEAD_DIM
            for at, ref in enumerate(packed):
                rows = slice((at * fold + turn) * piece, (at * fold + turn + 1) * piece)
                q_buf[head, rows, :HEAD_DIM] = ref[0, :, low : low + HEAD_DIM]
                k_buf[head, rows, :HEAD_DIM] = ref[1, :, low : low + HEAD_DIM]
                v_buf[head, rows, :HEAD_DIM] = ref[2, :, low : low + HEAD_DIM]
                q_buf[head, rows, HEAD_DIM:] = zeros
                k_buf[head, rows, HEAD_DIM:] = zeros
                v_buf[head, rows, HEAD_DIM:] = ones
    for at, out_ref in enumerate(outs):
        rows = slice(at * rows_each, (at + 1) * rows_each)
        allowed = ids_col_ref[rows, :] == ids_row_ref[...]
        for head in range(heads):
            scores = lax.dot_general(
                q_buf[head, rows, :],
                k_buf[head],
                (((1,), (1,)), ((), ())),
                preferred_element_type=jnp.float32,
            )
            scores = jnp.where(allowed, scores, -1e30)
            highest = jnp.max(scores, axis=-1, keepdims=True)
            weights = jnp.exp((scores - highest) * HEAD_DIM ** (-0.5)).astype(jnp.bfloat16)
            mixed = jnp.dot(weights, v_buf[head], preferred_element_type=jnp.float32)
            mixed = (mixed[:, :HEAD_DIM] / mixed[:, HEAD_DIM : HEAD_DIM + 1]).astype(jnp.bfloat16)
            for turn in range(fold):
                low = turn * part + head * HEAD_DIM
                out_ref[:, low : low + HEAD_DIM] = mixed[turn * piece : (turn + 1) * piece]


def project_kernel(members, groups, fold, me_ref, patch_ref, proj_ref, gain_ref, *refs):
    packed, (above_ref, below_ref, rows_buf, normed) = refs[:-4], refs[-4:]
    piece, wide = packed[0].shape
    part = wide // fold
    depth = groups * part
    residual = patch_ref[...].astype(jnp.float32)
    for shift in range(members):
        for group in range(groups):
            for turn in range(fold):
                rows_buf[
                    shift, turn * piece : (turn + 1) * piece, group * part : (group + 1) * part
                ] = packed[group * members + shift][:, turn * part : (turn + 1) * part]
        low = pl.multiple_of(lax.rem(me_ref[0] + shift, members) * depth, depth)
        residual += jnp.dot(
            rows_buf[shift], proj_ref[pl.ds(low, depth), :], preferred_element_type=jnp.float32
        )
    mean_square = jnp.mean(residual * residual, axis=-1, keepdims=True)
    states = residual * lax.rsqrt(mean_square + EPSILON) * gain_ref[...]
    half, width = above_ref.shape[0], residual.shape[1]
    for tile in range(width // LANES):
        normed[tile] = states[:, tile * LANES : (tile + 1) * LANES]
    for at in range(4):
        for tile in range(width // LANES):
            columns = slice(at * width + tile * LANES, at * width + (tile + 1) * LANES)
            for ref, low in ((above_ref, at), (below_ref, 4 * half + at)):
                ref[:, columns] = normed[tile, pl.ds(low, half, stride=4), :].astype(jnp.bfloat16)


def hidden_kernel(pieces, count, me_ref, *refs):
    blocks, refs = refs[:count], refs[count:]
    given, (hidden_ref, rows_buf, up_buf, acc, sem) = refs[: len(pieces)], refs[len(pieces) :]
    fetch(pieces, given, up_buf, sem)
    members, _, depth = rows_buf.shape
    half = blocks[0].shape[0]
    for at, block in enumerate(blocks):
        for k in range(members):
            rows_buf[k, at * half : (at + 1) * half, :] = block[:, k * depth : (k + 1) * depth]
    acc[...] = jnp.zeros_like(acc)

    def one_piece(mask, carry):
        arrive(up_buf, sem, mask)
        acc[...] += jnp.dot(
            rows_buf[me_ref[0] ^ mask], up_buf[mask], preferred_element_type=jnp.float32
        )
        return carry

    lax.fori_loop(0, members, one_piece, 0)
    total = acc[...]
    hidden_ref[...] = (0.5 * total * (1.0 + lax.erf(total * 0.5**0.5))).astype(jnp.bfloat16)


def sums_kernel(pieces, count, me_ref, early_ref, late_ref, *refs):
    given, refs = refs[: len(pieces)], refs[len(pieces) :]
    sums, (hidden_buf, down_buf, down_sem) = refs[:count], refs[count:]
    fetch(pieces, given, down_buf, down_sem)
    early = early_ref.shape[0]
    hidden_buf[:early] = early_ref[...]
    hidden_buf[early:] = late_ref[...]
    contract(me_ref, hidden_buf, down_buf, down_sem, sums)


def fetch(pieces, refs, buf, sem):
    for (mask, low, length), ref in zip(pieces, refs):
        pltpu.make_async_copy(ref, buf.at[mask, pl.ds(low, length)], sem.at[mask]).start()


def arrive(buf, sem, mask):
    pltpu.make_async_copy(buf.at[mask], buf.at[mask], sem.at[mask]).wait()


def contract(me_ref, hidden_ref, down_buf, down_sem, sums):
    count, wide, _ = down_buf.shape
    half = sums[0].shape[0]

    def one_piece(mask, carry):
        arrive(down_buf, down_sem, mask)
        product = lax.dot_general(
            hidden_ref[...],
            down_buf[mask],
            (((1,), (1,)), ((), ())),
            preferred_element_type=jnp.float32,
        ).astype(jnp.bfloat16)
        low = pl.multiple_of((me_ref[0] ^ mask) * wide, wide)
        for at, ref in enumerate(sums):
            ref[:, pl.ds(low, wide)] = product[at * half : (at + 1) * half]
        return carry

    lax.fori_loop(0, count, one_piece, 0)


def route_kernel(selector_ref, plus_ref, plus_own_ref, minus_ref, minus_own_ref, *outs):
    plus = plus_ref[...].astype(jnp.float32) + plus_own_ref[...].astype(jnp.float32)
    minus = minus_ref[...].astype(jnp.float32) + minus_own_ref[...].astype(jnp.float32)
    merged = jnp.concatenate([plus.astype(jnp.bfloat16), minus.astype(jnp.bfloat16)], axis=0)
    routed = jnp.dot(selector_ref[...], merged, preferred_element_type=jnp.float32).astype(
        jnp.bfloat16
    )
    each = outs[0].shape[0]
    for at, ref in enumerate(outs):
        ref[...] = routed[at * each : (at + 1) * each]


def line_up(arrived, rows_buf):
    each = arrived[0].shape[0]
    for at, ref in enumerate(arrived):
        rows_buf[at * each : (at + 1) * each, :] = ref[...]


def place_kernel(start, step, aliased, covered_ref, placement_ref, text_ref, *refs):
    refs = refs[1:] if aliased else refs
    arrived, (out_ref, rows_buf, before, result, in_sem, out_sem) = refs[:-6], refs[-6:]
    count, _, wide = before.shape

    def window(ref, at):
        return ref.at[:, pl.ds(at * step + start, wide)]

    reads = [
        pltpu.make_async_copy(window(text_ref, at), before.at[at], in_sem.at[at])
        for at in range(count)
    ]
    writes = [
        pltpu.make_async_copy(result.at[at], window(out_ref, at), out_sem.at[at])
        for at in range(count)
    ]
    for read in reads:
        read.start()
    line_up(arrived, rows_buf)
    covered = covered_ref[...] > 0
    for at in range(count):
        placed = jnp.dot(
            placement_ref[...],
            rows_buf[:, at * wide : (at + 1) * wide],
            preferred_element_type=jnp.float32,
        ).astype(jnp.bfloat16)
        reads[at].wait()
        result[at] = jnp.where(covered, placed, before[at])
        writes[at].start()
    for write in writes:
        write.wait()


def add(first, second):
    return (first.astype(jnp.float32) + second.astype(jnp.float32)).astype(jnp.bfloat16)


def ring(value, step):
    members = lax.axis_size("vit")
    return lax.ppermute(value, "vit", [(i, (i + step) % members) for i in range(members)])


def gather_pieces(value, direct=False):
    senders, rows = lax.axis_size("dp"), value.shape[0]
    side = 1
    while 2 * side * side < senders:
        side *= 2
    along_x, along_y = 2 * (side - 1), 2 * side * (side - 1)
    unit = 128 if rows >= 256 else 16
    cut = rows // 2 // unit * unit

    def swap(part, bit):
        low, array = part
        return low, lax.ppermute(array, "dp", [(i, i ^ bit) for i in range(senders)])

    def part_of(parts, top):
        if len(parts) == 2:
            return parts[0 if top else 1]
        array = parts[0][1]
        return (0, array[:cut]) if top else (cut, array[cut:])

    def high(mask):
        return 1 << (mask.bit_length() - 1)

    found = {0: [(0, value)]}
    for mask in range(2, senders, 2):
        x, y = mask & along_x, mask & along_y
        if x and y and direct:
            found[mask] = [swap(found[0][0], mask)]
        elif x and y:
            top = part_of(found[x | (y ^ high(y))], True)
            bottom = part_of(found[(x ^ high(x)) | y], False)
            found[mask] = [swap(top, high(y)), swap(bottom, high(x))]
        else:
            found[mask] = [swap(p, high(mask)) for p in found[mask ^ high(mask)]]
    for mask in range(1, senders, 2):
        found[mask] = [swap(p, 1) for p in found[mask ^ 1]]
    order = [(mask, low, a) for mask in range(senders) for low, a in found[mask]]
    return [(mask, low, a.shape[0]) for mask, low, a in order], [a for _, _, a in order]


def kernel(body, **options):
    return pl.pallas_call(body, **options)


def body(
    patch_states,
    queries,
    keys,
    values,
    out_proj,
    merge_gain,
    image_of_group,
    w_in,
    w_out,
    text_embeds,
    block_dest,
    placeholder_rows,
):
    row_count, feature_width = queries.shape
    members = lax.axis_size("vit")
    senders = lax.axis_size("dp")
    me = lax.axis_index("dp").astype(jnp.int32)[None]
    member = lax.axis_index("vit").astype(jnp.int32)
    heads = HEADS // members // GROUPS
    fold = fold_of(heads * HEAD_DIM)
    piece, packed_width = row_count // fold, heads * HEAD_DIM * fold
    vmem = pl.BlockSpec(memory_space=pltpu.VMEM)
    smem = pl.BlockSpec(memory_space=pltpu.SMEM)
    hbm = pl.BlockSpec(memory_space=pl.ANY)

    packed = kernel(
functools.partial(pack_kernel, members, GROUPS, fold),
        out_shape=[jax.ShapeDtypeStruct((3, piece, packed_width), jnp.bfloat16)]
        * (GROUPS * members),
        in_specs=[smem] + [vmem] * 3,
        out_specs=[vmem] * (GROUPS * members),
        scratch_shapes=[pltpu.VMEM((members, GROUPS, 3, piece, packed_width), jnp.bfloat16)],
    )(member[None], queries, keys, values)
    arrived = [
        [
            packed[g * members + s]
            if s == 0
            else ring(packed[g * members + s], s)
            for s in range(members)
        ]
        for g in range(GROUPS)
    ]

    image_ids = jnp.repeat(image_of_group[0], 4)
    shifts = lax.rem(member + members - jnp.arange(members, dtype=jnp.int32), members)
    image_ids = image_ids.reshape(members, row_count)[shifts].reshape(-1)
    blocks = block_dest.shape[1]
    block_height = row_count // 4 // blocks
    slots, text_rows = 2 * senders * block_height, text_embeds.shape[0]
    height = jnp.arange(block_height, dtype=jnp.int32)[None, :]
    destination = block_dest[0]
    positions = jnp.arange(blocks, dtype=jnp.int32)
    earlier = (destination[:, None] == destination[None, :]) & (
        positions[None, :] < positions[:, None]
    )
    slot_rank = jnp.sum(earlier.astype(jnp.int32), axis=1)
    slot_index = (destination ^ me) * 2 + slot_rank
    row_slots = (slot_index[:, None] * block_height + height).reshape(-1)
    selector = (jnp.arange(slots, dtype=jnp.int32)[:, None] == row_slots[None, :]).astype(
        jnp.bfloat16
    )
    others = jnp.arange(senders, dtype=jnp.int32) ^ me
    first_row = placeholder_rows.reshape(senders, 2)[others].reshape(-1)
    targets = jnp.where(first_row[:, None] >= 0, first_row[:, None] + height, -1).reshape(-1)
    placement = jnp.arange(text_rows, dtype=jnp.int32)[:, None] == targets[None, :]
    covered = jnp.any(placement, axis=1, keepdims=True).astype(jnp.int32)
    placement = placement.astype(jnp.bfloat16)

    ids_col, ids_row = image_ids[:, None], image_ids[None, :]
    returned = []
    for g in range(GROUPS):
        if g == GROUPS - 1:
            me, selector, placement, covered, ids_col, ids_row = lax.optimization_barrier(
                (me, selector, placement, covered, ids_col, ids_row)
            )
        attended = kernel(
functools.partial(attend_kernel, members, heads, fold),
            out_shape=[jax.ShapeDtypeStruct((piece, packed_width), jnp.bfloat16)] * members,
            in_specs=[vmem] * (2 + members),
            out_specs=[vmem] * members,
            scratch_shapes=[pltpu.VMEM((heads, row_count * members, LANES), jnp.bfloat16)] * 3,
            cost_estimate=pl.CostEstimate(
                flops=8 * heads * LANES * (row_count * members) ** 2,
                bytes_accessed=8 * row_count * feature_width,
                transcendentals=heads * (row_count * members) ** 2,
            ),
        )(ids_col, ids_row, *arrived[g])
        returned += [attended[s] if s == 0 else ring(attended[s], -s) for s in range(members)]

    half, merge_width = row_count // 8, 4 * feature_width
    above, below = kernel(
        functools.partial(project_kernel, members, GROUPS, fold),
        out_shape=[jax.ShapeDtypeStruct((half, merge_width), jnp.bfloat16)] * 2,
        in_specs=[smem] + [vmem] * (3 + GROUPS * members),
        out_specs=[vmem] * 2,
        scratch_shapes=[
            pltpu.VMEM((members, row_count, feature_width // members), jnp.bfloat16),
            pltpu.VMEM((feature_width // LANES, row_count, LANES), jnp.float32),
        ],
    )(member[None], patch_states, out_proj, merge_gain[None, :], *returned)

    rows = {("up", 0): above, ("low", 0): below}
    for step in range(1, members):
        above = ring(above, 1)
        below = ring(below, -1)
        rows["up", members - step] = above
        rows["low", step] = below
    late = [("up", 1), ("low", members - 1)]
    early = [name for name in rows if name not in late]

    units = w_out.shape[0] // LANES
    widths = [(units - max(1, units * 3 // 8)) * LANES, max(1, units * 3 // 8) * LANES]
    up_pieces, up_arrays = gather_pieces(w_in)
    down = [gather_pieces(w_out[: widths[0]]), gather_pieces(w_out[widths[0] :])]
    hid = w_in.shape[1]

    def weight_cost(count, *parts):
        size = hid * senders * sum(parts)
        return pl.CostEstimate(flops=2 * count * size, bytes_accessed=2 * size, transcendentals=0)

    hidden = []
    for names in (early, late):
        count = len(names)
        hidden.append(
            kernel(
                functools.partial(hidden_kernel, up_pieces, count),
                out_shape=jax.ShapeDtypeStruct((count * half, hid), jnp.bfloat16),
                in_specs=[smem] + [vmem] * count + [hbm] * len(up_pieces),
                out_specs=vmem,
                scratch_shapes=[
                    pltpu.VMEM((senders, count * half, w_in.shape[0]), jnp.bfloat16),
                    pltpu.VMEM((senders,) + w_in.shape, jnp.bfloat16),
                    pltpu.VMEM((count * half, hid), jnp.float32),
                    pltpu.SemaphoreType.DMA((senders,)),
                ],
                cost_estimate=weight_cost(count * half, w_in.shape[0]),
            )(me, *[rows[name] for name in names], *up_arrays)
        )
    count = 2 * members
    sums = []
    for wide, (pieces, arrays) in zip(widths, down):
        results = kernel(
            functools.partial(sums_kernel, pieces, count),
            out_shape=[jax.ShapeDtypeStruct((half, senders * wide), jnp.bfloat16)] * count,
            in_specs=[smem, vmem, vmem] + [hbm] * len(pieces),
            out_specs=[vmem] * count,
            scratch_shapes=[
                pltpu.VMEM((count * half, hid), jnp.bfloat16),
                pltpu.VMEM((senders, wide, hid), jnp.bfloat16),
                pltpu.SemaphoreType.DMA((senders,)),
            ],
            cost_estimate=weight_cost(count * half, wide),
        )(me, *hidden, *arrays)
        sums.append(dict(zip(early + late, results)))

    text = None
    for c, wide in enumerate(widths):
        width = senders * wide
        plus, minus = sums[c]["up", members - 1], sums[c]["low", 1]
        for step in range(1, members):
            if step > 1:
                plus = add(plus, sums[c]["up", members - step])
                minus = add(minus, sums[c]["low", step])
            plus = ring(plus, 1)
            minus = ring(minus, -1)
        each = 2 * block_height
        routed = kernel(
            route_kernel,
            out_shape=[jax.ShapeDtypeStruct((each, width), jnp.bfloat16)] * senders,
            in_specs=[vmem] * 5,
            out_specs=[vmem] * senders,
        )(selector, plus, sums[c]["up", 0], minus, sums[c]["low", 0])
        incoming = [routed[0]]
        for mask in range(1, senders):
            incoming.append(
                lax.ppermute(routed[mask], "dp", [(i, i ^ mask) for i in range(senders)])
            )
        before = [text] if c else []
        text = kernel(
            functools.partial(place_kernel, sum(widths[:c]), sum(widths), c > 0),
            out_shape=jax.ShapeDtypeStruct(text_embeds.shape, jnp.bfloat16),
            in_specs=[vmem, vmem, hbm] + [hbm] * len(before) + [vmem] * senders,
            out_specs=hbm,
            scratch_shapes=[
                pltpu.VMEM((slots, width), jnp.bfloat16),
                pltpu.VMEM((senders, text_rows, wide), jnp.bfloat16),
                pltpu.VMEM((senders, text_rows, wide), jnp.bfloat16),
                pltpu.SemaphoreType.DMA((senders,)),
                pltpu.SemaphoreType.DMA((senders,)),
            ],
            input_output_aliases={3: 0} if c else {},
        )(covered, placement, text_embeds, *before, *incoming)
    return text


def solution(mesh):
    placed = (
        P(("dp", "vit"), None),
        P(("dp", "vit"), None),
        P(("dp", "vit"), None),
        P(("dp", "vit"), None),
        P(),
        P(),
        P("dp", None),
        P("dp", "vit"),
        P("dp", "vit"),
        P(("dp", "vit"), None),
        P(("dp", "vit"), None),
        P(("dp", "vit"), None),
    )

    return jax.shard_map(
        body, mesh=mesh, in_specs=placed, out_specs=P(("dp", "vit"), None), check_vma=False
    )
```

```python
import functools

import jax
import jax.numpy as jnp
from jax import lax
from jax.experimental import pallas as pl
from jax.experimental.pallas import tpu as pltpu
from jax.sharding import PartitionSpec as P

HEADS = 16
HEAD_DIM = 80
EPSILON = 1e-06
LANES = 128
GROUPS = 2


def fold_of(width):
    fold = 1
    while (width * fold) % LANES:
        fold *= 2
    return fold


def pack_kernel(members, groups, fold, me_ref, q_ref, k_ref, v_ref, *refs):
    outs, buf = refs[:-1], refs[-1]
    rows, width = q_ref.shape
    part, piece = width // (members * groups), rows // fold
    for at, ref in enumerate((q_ref, k_ref, v_ref)):
        for member in range(members):
            for group in range(groups):
                low = (member * groups + group) * part
                for turn in range(fold):
                    buf[member, group, at, :, turn * part : (turn + 1) * part] = ref[
                        turn * piece : (turn + 1) * piece, low : low + part
                    ]
    for group in range(groups):
        for shift in range(members):
            outs[group * members + shift][...] = buf[lax.rem(me_ref[0] + shift, members), group]


def attend_kernel(members, heads, fold, ids_col_ref, ids_row_ref, *refs):
    packed, outs, (q_buf, k_buf, v_buf) = refs[:members], refs[members:-3], refs[-3:]
    _, piece, _ = packed[0].shape
    part, rows_each = heads * HEAD_DIM, piece * fold
    lane = lax.broadcasted_iota(jnp.int32, (piece, LANES - HEAD_DIM), 1)
    ones = jnp.where(lane == 0, 1.0, 0.0).astype(jnp.bfloat16)
    zeros = jnp.zeros((piece, LANES - HEAD_DIM), jnp.bfloat16)
    for head in range(heads):
        for turn in range(fold):
            low = turn * part + head * HEAD_DIM
            for at, ref in enumerate(packed):
                rows = slice((at * fold + turn) * piece, (at * fold + turn + 1) * piece)
                q_buf[head, rows, :HEAD_DIM] = ref[0, :, low : low + HEAD_DIM]
                k_buf[head, rows, :HEAD_DIM] = ref[1, :, low : low + HEAD_DIM]
                v_buf[head, rows, :HEAD_DIM] = ref[2, :, low : low + HEAD_DIM]
                q_buf[head, rows, HEAD_DIM:] = zeros
                k_buf[head, rows, HEAD_DIM:] = zeros
                v_buf[head, rows, HEAD_DIM:] = ones
    for at, out_ref in enumerate(outs):
        rows = slice(at * rows_each, (at + 1) * rows_each)
        allowed = ids_col_ref[rows, :] == ids_row_ref[...]
        for head in range(heads):
            scores = lax.dot_general(
                q_buf[head, rows, :],
                k_buf[head],
                (((1,), (1,)), ((), ())),
                preferred_element_type=jnp.float32,
            )
            scores = jnp.where(allowed, scores, -1e30)
            highest = jnp.max(scores, axis=-1, keepdims=True)
            weights = jnp.exp((scores - highest) * HEAD_DIM ** (-0.5)).astype(jnp.bfloat16)
            mixed = jnp.dot(weights, v_buf[head], preferred_element_type=jnp.float32)
            mixed = (mixed[:, :HEAD_DIM] / mixed[:, HEAD_DIM : HEAD_DIM + 1]).astype(jnp.bfloat16)
            for turn in range(fold):
                low = turn * part + head * HEAD_DIM
                out_ref[:, low : low + HEAD_DIM] = mixed[turn * piece : (turn + 1) * piece]


def project_kernel(members, groups, fold, me_ref, patch_ref, proj_ref, gain_ref, *refs):
    packed, (above_ref, below_ref, rows_buf, normed) = refs[:-4], refs[-4:]
    piece, wide = packed[0].shape
    part = wide // fold
    depth = groups * part
    residual = patch_ref[...].astype(jnp.float32)
    for shift in range(members):
        for group in range(groups):
            for turn in range(fold):
                rows_buf[
                    shift, turn * piece : (turn + 1) * piece, group * part : (group + 1) * part
                ] = packed[group * members + shift][:, turn * part : (turn + 1) * part]
        low = pl.multiple_of(lax.rem(me_ref[0] + shift, members) * depth, depth)
        residual += jnp.dot(
            rows_buf[shift], proj_ref[pl.ds(low, depth), :], preferred_element_type=jnp.float32
        )
    mean_square = jnp.mean(residual * residual, axis=-1, keepdims=True)
    states = residual * lax.rsqrt(mean_square + EPSILON) * gain_ref[...]
    half, width = above_ref.shape[0], residual.shape[1]
    for tile in range(width // LANES):
        normed[tile] = states[:, tile * LANES : (tile + 1) * LANES]
    for at in range(4):
        for tile in range(width // LANES):
            columns = slice(at * width + tile * LANES, at * width + (tile + 1) * LANES)
            for ref, low in ((above_ref, at), (below_ref, 4 * half + at)):
                ref[:, columns] = normed[tile, pl.ds(low, half, stride=4), :].astype(jnp.bfloat16)


def hidden_kernel(pieces, count, me_ref, *refs):
    blocks, refs = refs[:count], refs[count:]
    given, (hidden_ref, rows_buf, up_buf, acc, sem) = refs[: len(pieces)], refs[len(pieces) :]
    fetch(pieces, given, up_buf, sem)
    members, _, depth = rows_buf.shape
    half = blocks[0].shape[0]
    for at, block in enumerate(blocks):
        for k in range(members):
            rows_buf[k, at * half : (at + 1) * half, :] = block[:, k * depth : (k + 1) * depth]
    acc[...] = jnp.zeros_like(acc)

    def one_piece(mask, carry):
        arrive(up_buf, sem, mask)
        acc[...] += jnp.dot(
            rows_buf[me_ref[0] ^ mask], up_buf[mask], preferred_element_type=jnp.float32
        )
        return carry

    lax.fori_loop(0, members, one_piece, 0)
    total = acc[...]
    hidden_ref[...] = (0.5 * total * (1.0 + lax.erf(total * 0.5**0.5))).astype(jnp.bfloat16)


def sums_kernel(pieces, counts, me_ref, *refs):
    given, refs = refs[: len(counts)], refs[len(counts) :]
    arrays, refs = refs[: len(pieces)], refs[len(pieces) :]
    sums, (hidden_buf, down_buf, down_sem) = refs[: sum(counts)], refs[sum(counts) :]
    fetch(pieces, arrays, down_buf, down_sem)
    low = 0
    for ref in given:
        hidden_buf[low : low + ref.shape[0]] = ref[...]
        low += ref.shape[0]
    contract(me_ref, hidden_buf, down_buf, down_sem, sums)


def fetch(pieces, refs, buf, sem):
    for (mask, low, length), ref in zip(pieces, refs):
        pltpu.make_async_copy(ref, buf.at[mask, pl.ds(low, length)], sem.at[mask]).start()


def arrive(buf, sem, mask):
    pltpu.make_async_copy(buf.at[mask], buf.at[mask], sem.at[mask]).wait()


def contract(me_ref, hidden_ref, down_buf, down_sem, sums):
    count, wide, _ = down_buf.shape
    half = sums[0].shape[0]

    def one_piece(mask, carry):
        arrive(down_buf, down_sem, mask)
        product = lax.dot_general(
            hidden_ref[...],
            down_buf[mask],
            (((1,), (1,)), ((), ())),
            preferred_element_type=jnp.float32,
        ).astype(jnp.bfloat16)
        low = pl.multiple_of((me_ref[0] ^ mask) * wide, wide)
        for at, ref in enumerate(sums):
            ref[:, pl.ds(low, wide)] = product[at * half : (at + 1) * half]
        return carry

    lax.fori_loop(0, count, one_piece, 0)


def route_kernel(selector_ref, plus_ref, plus_own_ref, minus_ref, minus_own_ref, *outs):
    plus = plus_ref[...].astype(jnp.float32) + plus_own_ref[...].astype(jnp.float32)
    minus = minus_ref[...].astype(jnp.float32) + minus_own_ref[...].astype(jnp.float32)
    merged = jnp.concatenate([plus.astype(jnp.bfloat16), minus.astype(jnp.bfloat16)], axis=0)
    routed = jnp.dot(selector_ref[...], merged, preferred_element_type=jnp.float32).astype(
        jnp.bfloat16
    )
    each = outs[0].shape[0]
    for at, ref in enumerate(outs):
        ref[...] = routed[at * each : (at + 1) * each]


def line_up(arrived, rows_buf):
    each = arrived[0].shape[0]
    for at, ref in enumerate(arrived):
        rows_buf[at * each : (at + 1) * each, :] = ref[...]


def place_kernel(start, step, aliased, covered_ref, placement_ref, text_ref, *refs):
    refs = refs[1:] if aliased else refs
    arrived, (out_ref, rows_buf, before, result, in_sem, out_sem) = refs[:-6], refs[-6:]
    count, _, wide = before.shape

    def window(ref, at):
        return ref.at[:, pl.ds(at * step + start, wide)]

    reads = [
        pltpu.make_async_copy(window(text_ref, at), before.at[at], in_sem.at[at])
        for at in range(count)
    ]
    writes = [
        pltpu.make_async_copy(result.at[at], window(out_ref, at), out_sem.at[at])
        for at in range(count)
    ]
    for read in reads:
        read.start()
    line_up(arrived, rows_buf)
    covered = covered_ref[...] > 0
    for at in range(count):
        placed = jnp.dot(
            placement_ref[...],
            rows_buf[:, at * wide : (at + 1) * wide],
            preferred_element_type=jnp.float32,
        ).astype(jnp.bfloat16)
        reads[at].wait()
        result[at] = jnp.where(covered, placed, before[at])
        writes[at].start()
    for write in writes:
        write.wait()


def add(first, second):
    return (first.astype(jnp.float32) + second.astype(jnp.float32)).astype(jnp.bfloat16)


def ring(value, step):
    members = lax.axis_size("vit")
    return lax.ppermute(value, "vit", [(i, (i + step) % members) for i in range(members)])


def gather_pieces(value, direct=False):
    senders, rows = lax.axis_size("dp"), value.shape[0]
    side = 1
    while 2 * side * side < senders:
        side *= 2
    along_x, along_y = 2 * (side - 1), 2 * side * (side - 1)
    unit = 128 if rows >= 256 else 16
    cut = rows // 2 // unit * unit

    def swap(part, bit):
        low, array = part
        return low, lax.ppermute(array, "dp", [(i, i ^ bit) for i in range(senders)])

    def part_of(parts, top):
        if len(parts) == 2:
            return parts[0 if top else 1]
        array = parts[0][1]
        return (0, array[:cut]) if top else (cut, array[cut:])

    def high(mask):
        return 1 << (mask.bit_length() - 1)

    found = {0: [(0, value)]}
    for mask in range(2, senders, 2):
        x, y = mask & along_x, mask & along_y
        if x and y and direct:
            found[mask] = [swap(found[0][0], mask)]
        elif x and y:
            top = part_of(found[x | (y ^ high(y))], True)
            bottom = part_of(found[(x ^ high(x)) | y], False)
            found[mask] = [swap(top, high(y)), swap(bottom, high(x))]
        else:
            found[mask] = [swap(p, high(mask)) for p in found[mask ^ high(mask)]]
    for mask in range(1, senders, 2):
        found[mask] = [swap(p, 1) for p in found[mask ^ 1]]
    order = [(mask, low, a) for mask in range(senders) for low, a in found[mask]]
    return [(mask, low, a.shape[0]) for mask, low, a in order], [a for _, _, a in order]


def kernel(body, **options):
    return pl.pallas_call(body, **options)


def body(
    patch_states,
    queries,
    keys,
    values,
    out_proj,
    merge_gain,
    image_of_group,
    w_in,
    w_out,
    text_embeds,
    block_dest,
    placeholder_rows,
):
    row_count, feature_width = queries.shape
    members = lax.axis_size("vit")
    senders = lax.axis_size("dp")
    me = lax.axis_index("dp").astype(jnp.int32)[None]
    member = lax.axis_index("vit").astype(jnp.int32)
    heads = HEADS // members // GROUPS
    fold = fold_of(heads * HEAD_DIM)
    piece, packed_width = row_count // fold, heads * HEAD_DIM * fold
    vmem = pl.BlockSpec(memory_space=pltpu.VMEM)
    smem = pl.BlockSpec(memory_space=pltpu.SMEM)
    hbm = pl.BlockSpec(memory_space=pl.ANY)

    packed = kernel(
functools.partial(pack_kernel, members, GROUPS, fold),
        out_shape=[jax.ShapeDtypeStruct((3, piece, packed_width), jnp.bfloat16)]
        * (GROUPS * members),
        in_specs=[smem] + [vmem] * 3,
        out_specs=[vmem] * (GROUPS * members),
        scratch_shapes=[pltpu.VMEM((members, GROUPS, 3, piece, packed_width), jnp.bfloat16)],
    )(member[None], queries, keys, values)
    arrived = [
        [
            packed[g * members + s]
            if s == 0
            else ring(packed[g * members + s], s)
            for s in range(members)
        ]
        for g in range(GROUPS)
    ]

    image_ids = jnp.repeat(image_of_group[0], 4)
    shifts = lax.rem(member + members - jnp.arange(members, dtype=jnp.int32), members)
    image_ids = image_ids.reshape(members, row_count)[shifts].reshape(-1)
    blocks = block_dest.shape[1]
    block_height = row_count // 4 // blocks
    slots, text_rows = 2 * senders * block_height, text_embeds.shape[0]
    height = jnp.arange(block_height, dtype=jnp.int32)[None, :]
    destination = block_dest[0]
    positions = jnp.arange(blocks, dtype=jnp.int32)
    earlier = (destination[:, None] == destination[None, :]) & (
        positions[None, :] < positions[:, None]
    )
    slot_rank = jnp.sum(earlier.astype(jnp.int32), axis=1)
    slot_index = (destination ^ me) * 2 + slot_rank
    row_slots = (slot_index[:, None] * block_height + height).reshape(-1)
    selector = (jnp.arange(slots, dtype=jnp.int32)[:, None] == row_slots[None, :]).astype(
        jnp.bfloat16
    )
    others = jnp.arange(senders, dtype=jnp.int32) ^ me
    first_row = placeholder_rows.reshape(senders, 2)[others].reshape(-1)
    targets = jnp.where(first_row[:, None] >= 0, first_row[:, None] + height, -1).reshape(-1)
    placement = jnp.arange(text_rows, dtype=jnp.int32)[:, None] == targets[None, :]
    covered = jnp.any(placement, axis=1, keepdims=True).astype(jnp.int32)
    placement = placement.astype(jnp.bfloat16)

    ids_col, ids_row = image_ids[:, None], image_ids[None, :]
    returned = []
    for g in range(GROUPS):
        if g == GROUPS - 1:
            me, selector, placement, covered, ids_col, ids_row = lax.optimization_barrier(
                (me, selector, placement, covered, ids_col, ids_row)
            )
        attended = kernel(
functools.partial(attend_kernel, members, heads, fold),
            out_shape=[jax.ShapeDtypeStruct((piece, packed_width), jnp.bfloat16)] * members,
            in_specs=[vmem] * (2 + members),
            out_specs=[vmem] * members,
            scratch_shapes=[pltpu.VMEM((heads, row_count * members, LANES), jnp.bfloat16)] * 3,
            cost_estimate=pl.CostEstimate(
                flops=8 * heads * LANES * (row_count * members) ** 2,
                bytes_accessed=8 * row_count * feature_width,
                transcendentals=heads * (row_count * members) ** 2,
            ),
        )(ids_col, ids_row, *arrived[g])
        returned += [attended[s] if s == 0 else ring(attended[s], -s) for s in range(members)]

    half, merge_width = row_count // 8, 4 * feature_width
    above, below = kernel(
        functools.partial(project_kernel, members, GROUPS, fold),
        out_shape=[jax.ShapeDtypeStruct((half, merge_width), jnp.bfloat16)] * 2,
        in_specs=[smem] + [vmem] * (3 + GROUPS * members),
        out_specs=[vmem] * 2,
        scratch_shapes=[
            pltpu.VMEM((members, row_count, feature_width // members), jnp.bfloat16),
            pltpu.VMEM((feature_width // LANES, row_count, LANES), jnp.float32),
        ],
    )(member[None], patch_states, out_proj, merge_gain[None, :], *returned)

    rows = {("up", 0): above, ("low", 0): below}
    for step in range(1, members):
        above = ring(above, 1)
        below = ring(below, -1)
        rows["up", members - step] = above
        rows["low", step] = below
    late = [("up", 1), ("low", members - 1)]
    early = [name for name in rows if name not in late]

    units = w_out.shape[0] // LANES
    widths = [(units - max(1, units * 3 // 8)) * LANES, max(1, units * 3 // 8) * LANES]
    up_pieces, up_arrays = gather_pieces(w_in)
    down = [gather_pieces(w_out[: widths[0]]), gather_pieces(w_out[widths[0] :])]
    hid = w_in.shape[1]

    def weight_cost(count, *parts):
        size = hid * senders * sum(parts)
        return pl.CostEstimate(flops=2 * count * size, bytes_accessed=2 * size, transcendentals=0)

    hidden = []
    for names in (early, late):
        count = len(names)
        hidden.append(
            kernel(
                functools.partial(hidden_kernel, up_pieces, count),
                out_shape=jax.ShapeDtypeStruct((count * half, hid), jnp.bfloat16),
                in_specs=[smem] + [vmem] * count + [hbm] * len(up_pieces),
                out_specs=vmem,
                scratch_shapes=[
                    pltpu.VMEM((senders, count * half, w_in.shape[0]), jnp.bfloat16),
                    pltpu.VMEM((senders,) + w_in.shape, jnp.bfloat16),
                    pltpu.VMEM((count * half, hid), jnp.float32),
                    pltpu.SemaphoreType.DMA((senders,)),
                ],
                cost_estimate=weight_cost(count * half, w_in.shape[0]),
            )(me, *[rows[name] for name in names], *up_arrays)
        )
    sums = [{}, {}]
    for c, given in ((0, (0,)), (0, (1,)), (1, (0, 1))):
        names = [(early, late)[at] for at in given]
        count = sum(map(len, names))
        wide, (pieces, arrays) = widths[c], down[c]
        results = kernel(
            functools.partial(sums_kernel, pieces, [len(each) for each in names]),
            out_shape=[jax.ShapeDtypeStruct((half, senders * wide), jnp.bfloat16)] * count,
            in_specs=[smem] + [vmem] * len(given) + [hbm] * len(pieces),
            out_specs=[vmem] * count,
            scratch_shapes=[
                pltpu.VMEM((count * half, hid), jnp.bfloat16),
                pltpu.VMEM((senders, wide, hid), jnp.bfloat16),
                pltpu.SemaphoreType.DMA((senders,)),
            ],
            cost_estimate=weight_cost(count * half, wide),
        )(me, *[hidden[at] for at in given], *arrays)
        sums[c].update(zip(sum(names, []), results))

    text = None
    for c, wide in enumerate(widths):
        width = senders * wide
        plus, minus = sums[c]["up", members - 1], sums[c]["low", 1]
        for step in range(1, members):
            if step > 1:
                plus = add(plus, sums[c]["up", members - step])
                minus = add(minus, sums[c]["low", step])
            plus = ring(plus, 1)
            minus = ring(minus, -1)
        each = 2 * block_height
        routed = kernel(
            route_kernel,
            out_shape=[jax.ShapeDtypeStruct((each, width), jnp.bfloat16)] * senders,
            in_specs=[vmem] * 5,
            out_specs=[vmem] * senders,
        )(selector, plus, sums[c]["up", 0], minus, sums[c]["low", 0])
        incoming = [routed[0]]
        for mask in range(1, senders):
            incoming.append(
                lax.ppermute(routed[mask], "dp", [(i, i ^ mask) for i in range(senders)])
            )
        before = [text] if c else []
        text = kernel(
            functools.partial(place_kernel, sum(widths[:c]), sum(widths), c > 0),
            out_shape=jax.ShapeDtypeStruct(text_embeds.shape, jnp.bfloat16),
            in_specs=[vmem, vmem, hbm] + [hbm] * len(before) + [vmem] * senders,
            out_specs=hbm,
            scratch_shapes=[
                pltpu.VMEM((slots, width), jnp.bfloat16),
                pltpu.VMEM((senders, text_rows, wide), jnp.bfloat16),
                pltpu.VMEM((senders, text_rows, wide), jnp.bfloat16),
                pltpu.SemaphoreType.DMA((senders,)),
                pltpu.SemaphoreType.DMA((senders,)),
            ],
            input_output_aliases={3: 0} if c else {},
        )(covered, placement, text_embeds, *before, *incoming)
    return text


def solution(mesh):
    placed = (
        P(("dp", "vit"), None),
        P(("dp", "vit"), None),
        P(("dp", "vit"), None),
        P(("dp", "vit"), None),
        P(),
        P(),
        P("dp", None),
        P("dp", "vit"),
        P("dp", "vit"),
        P(("dp", "vit"), None),
        P(("dp", "vit"), None),
        P(("dp", "vit"), None),
    )

    return jax.shard_map(
        body, mesh=mesh, in_specs=placed, out_specs=P(("dp", "vit"), None), check_vma=False
    )
```

```python
import functools

import jax
import jax.numpy as jnp
from jax import lax
from jax.experimental import pallas as pl
from jax.experimental.pallas import tpu as pltpu
from jax.sharding import PartitionSpec as P

HEADS = 16
HEAD_DIM = 80
EPSILON = 1e-06
LANES = 128
GROUPS = 2


def fold_of(width):
    fold = 1
    while (width * fold) % LANES:
        fold *= 2
    return fold


def pack_kernel(members, groups, fold, me_ref, q_ref, k_ref, v_ref, *refs):
    outs, buf = refs[:-1], refs[-1]
    rows, width = q_ref.shape
    part, piece = width // (members * groups), rows // fold
    for at, ref in enumerate((q_ref, k_ref, v_ref)):
        for member in range(members):
            for group in range(groups):
                low = (member * groups + group) * part
                for turn in range(fold):
                    buf[member, group, at, :, turn * part : (turn + 1) * part] = ref[
                        turn * piece : (turn + 1) * piece, low : low + part
                    ]
    for group in range(groups):
        for shift in range(members):
            outs[group * members + shift][...] = buf[lax.rem(me_ref[0] + shift, members), group]


def attend_kernel(members, heads, fold, ids_col_ref, ids_row_ref, *refs):
    packed, outs, (q_buf, k_buf, v_buf) = refs[:members], refs[members:-3], refs[-3:]
    _, piece, _ = packed[0].shape
    part, rows_each = heads * HEAD_DIM, piece * fold
    lane = lax.broadcasted_iota(jnp.int32, (piece, LANES - HEAD_DIM), 1)
    ones = jnp.where(lane == 0, 1.0, 0.0).astype(jnp.bfloat16)
    zeros = jnp.zeros((piece, LANES - HEAD_DIM), jnp.bfloat16)
    for head in range(heads):
        for turn in range(fold):
            low = turn * part + head * HEAD_DIM
            for at, ref in enumerate(packed):
                rows = slice((at * fold + turn) * piece, (at * fold + turn + 1) * piece)
                q_buf[head, rows, :HEAD_DIM] = ref[0, :, low : low + HEAD_DIM]
                k_buf[head, rows, :HEAD_DIM] = ref[1, :, low : low + HEAD_DIM]
                v_buf[head, rows, :HEAD_DIM] = ref[2, :, low : low + HEAD_DIM]
                q_buf[head, rows, HEAD_DIM:] = zeros
                k_buf[head, rows, HEAD_DIM:] = zeros
                v_buf[head, rows, HEAD_DIM:] = ones
    for at, out_ref in enumerate(outs):
        rows = slice(at * rows_each, (at + 1) * rows_each)
        allowed = ids_col_ref[rows, :] == ids_row_ref[...]
        for head in range(heads):
            scores = lax.dot_general(
                q_buf[head, rows, :],
                k_buf[head],
                (((1,), (1,)), ((), ())),
                preferred_element_type=jnp.float32,
            )
            scores = jnp.where(allowed, scores, -1e30)
            highest = jnp.max(scores, axis=-1, keepdims=True)
            weights = jnp.exp((scores - highest) * HEAD_DIM ** (-0.5)).astype(jnp.bfloat16)
            mixed = jnp.dot(weights, v_buf[head], preferred_element_type=jnp.float32)
            mixed = (mixed[:, :HEAD_DIM] / mixed[:, HEAD_DIM : HEAD_DIM + 1]).astype(jnp.bfloat16)
            for turn in range(fold):
                low = turn * part + head * HEAD_DIM
                out_ref[:, low : low + HEAD_DIM] = mixed[turn * piece : (turn + 1) * piece]


def project_kernel(members, groups, fold, me_ref, patch_ref, proj_ref, gain_ref, *refs):
    packed, (above_ref, below_ref, rows_buf, normed) = refs[:-4], refs[-4:]
    piece, wide = packed[0].shape
    part = wide // fold
    depth = groups * part
    residual = patch_ref[...].astype(jnp.float32)
    for shift in range(members):
        for group in range(groups):
            for turn in range(fold):
                rows_buf[
                    shift, turn * piece : (turn + 1) * piece, group * part : (group + 1) * part
                ] = packed[group * members + shift][:, turn * part : (turn + 1) * part]
        low = pl.multiple_of(lax.rem(me_ref[0] + shift, members) * depth, depth)
        residual += jnp.dot(
            rows_buf[shift], proj_ref[pl.ds(low, depth), :], preferred_element_type=jnp.float32
        )
    mean_square = jnp.mean(residual * residual, axis=-1, keepdims=True)
    states = residual * lax.rsqrt(mean_square + EPSILON) * gain_ref[...]
    half, width = above_ref.shape[0], residual.shape[1]
    for tile in range(width // LANES):
        normed[tile] = states[:, tile * LANES : (tile + 1) * LANES]
    for at in range(4):
        for tile in range(width // LANES):
            columns = slice(at * width + tile * LANES, at * width + (tile + 1) * LANES)
            for ref, low in ((above_ref, at), (below_ref, 4 * half + at)):
                ref[:, columns] = normed[tile, pl.ds(low, half, stride=4), :].astype(jnp.bfloat16)


def hidden_kernel(pieces, count, me_ref, *refs):
    blocks, refs = refs[:count], refs[count:]
    given, (hidden_ref, rows_buf, up_buf, acc, sem) = refs[: len(pieces)], refs[len(pieces) :]
    fetch(pieces, given, up_buf, sem)
    members, _, depth = rows_buf.shape
    half = blocks[0].shape[0]
    for at, block in enumerate(blocks):
        for k in range(members):
            rows_buf[k, at * half : (at + 1) * half, :] = block[:, k * depth : (k + 1) * depth]
    acc[...] = jnp.zeros_like(acc)

    def one_piece(mask, carry):
        arrive(up_buf, sem, mask)
        acc[...] += jnp.dot(
            rows_buf[me_ref[0] ^ mask], up_buf[mask], preferred_element_type=jnp.float32
        )
        return carry

    lax.fori_loop(0, members, one_piece, 0)
    total = acc[...]
    hidden_ref[...] = (0.5 * total * (1.0 + lax.erf(total * 0.5**0.5))).astype(jnp.bfloat16)


def sums_kernel(pieces, counts, me_ref, *refs):
    given, refs = refs[: len(counts)], refs[len(counts) :]
    arrays, refs = refs[: len(pieces)], refs[len(pieces) :]
    sums, (hidden_buf, down_buf, down_sem) = refs[: sum(counts)], refs[sum(counts) :]
    fetch(pieces, arrays, down_buf, down_sem)
    low = 0
    for ref in given:
        hidden_buf[low : low + ref.shape[0]] = ref[...]
        low += ref.shape[0]
    contract(me_ref, hidden_buf, down_buf, down_sem, sums)


def fetch(pieces, refs, buf, sem):
    for (mask, low, length), ref in zip(pieces, refs):
        pltpu.make_async_copy(ref, buf.at[mask, pl.ds(low, length)], sem.at[mask]).start()


def arrive(buf, sem, mask):
    pltpu.make_async_copy(buf.at[mask], buf.at[mask], sem.at[mask]).wait()


def contract(me_ref, hidden_ref, down_buf, down_sem, sums):
    count, wide, _ = down_buf.shape
    half = sums[0].shape[0]

    def one_piece(mask, carry):
        arrive(down_buf, down_sem, mask)
        product = lax.dot_general(
            hidden_ref[...],
            down_buf[mask],
            (((1,), (1,)), ((), ())),
            preferred_element_type=jnp.float32,
        ).astype(jnp.bfloat16)
        low = pl.multiple_of((me_ref[0] ^ mask) * wide, wide)
        for at, ref in enumerate(sums):
            ref[:, pl.ds(low, wide)] = product[at * half : (at + 1) * half]
        return carry

    lax.fori_loop(0, count, one_piece, 0)


def route_kernel(selector_ref, plus_ref, plus_own_ref, minus_ref, minus_own_ref, *outs):
    plus = plus_ref[...].astype(jnp.float32) + plus_own_ref[...].astype(jnp.float32)
    minus = minus_ref[...].astype(jnp.float32) + minus_own_ref[...].astype(jnp.float32)
    merged = jnp.concatenate([plus.astype(jnp.bfloat16), minus.astype(jnp.bfloat16)], axis=0)
    routed = jnp.dot(selector_ref[...], merged, preferred_element_type=jnp.float32).astype(
        jnp.bfloat16
    )
    each = outs[0].shape[0]
    for at, ref in enumerate(outs):
        ref[...] = routed[at * each : (at + 1) * each]


def line_up(arrived, rows_buf):
    each = arrived[0].shape[0]
    for at, ref in enumerate(arrived):
        rows_buf[at * each : (at + 1) * each, :] = ref[...]


def place_kernel(start, step, aliased, covered_ref, placement_ref, text_ref, *refs):
    refs = refs[1:] if aliased else refs
    arrived, (out_ref, rows_buf, before, result, in_sem, out_sem) = refs[:-6], refs[-6:]
    count, _, wide = before.shape

    def window(ref, at):
        return ref.at[:, pl.ds(at * step + start, wide)]

    reads = [
        pltpu.make_async_copy(window(text_ref, at), before.at[at], in_sem.at[at])
        for at in range(count)
    ]
    writes = [
        pltpu.make_async_copy(result.at[at], window(out_ref, at), out_sem.at[at])
        for at in range(count)
    ]
    for read in reads:
        read.start()
    line_up(arrived, rows_buf)
    covered = covered_ref[...] > 0
    for at in range(count):
        placed = jnp.dot(
            placement_ref[...],
            rows_buf[:, at * wide : (at + 1) * wide],
            preferred_element_type=jnp.float32,
        ).astype(jnp.bfloat16)
        reads[at].wait()
        result[at] = jnp.where(covered, placed, before[at])
        writes[at].start()
    for write in writes:
        write.wait()


def add(first, second):
    return (first.astype(jnp.float32) + second.astype(jnp.float32)).astype(jnp.bfloat16)


def shift(value, step):
    members = lax.axis_size("vit")
    return lax.ppermute(value, "vit", [(i, (i + step) % members) for i in range(members)])


def ring(value, step):
    members = lax.axis_size("vit")
    order = [0, *range(1, members, 2), *reversed(range(2, members, 2))]
    pairs = [(order[i], order[(i + step) % members]) for i in range(members)]
    return lax.ppermute(value, "vit", pairs)


def gather_pieces(value, direct=False):
    senders, rows = lax.axis_size("dp"), value.shape[0]
    side = 1
    while 2 * side * side < senders:
        side *= 2
    along_x, along_y = 2 * (side - 1), 2 * side * (side - 1)
    unit = 128 if rows >= 256 else 16
    cut = rows // 2 // unit * unit

    def swap(part, bit):
        low, array = part
        return low, lax.ppermute(array, "dp", [(i, i ^ bit) for i in range(senders)])

    def part_of(parts, top):
        if len(parts) == 2:
            return parts[0 if top else 1]
        array = parts[0][1]
        return (0, array[:cut]) if top else (cut, array[cut:])

    def high(mask):
        return 1 << (mask.bit_length() - 1)

    found = {0: [(0, value)]}
    for mask in range(2, senders, 2):
        x, y = mask & along_x, mask & along_y
        if x and y and direct:
            found[mask] = [swap(found[0][0], mask)]
        elif x and y:
            top = part_of(found[x | (y ^ high(y))], True)
            bottom = part_of(found[(x ^ high(x)) | y], False)
            found[mask] = [swap(top, high(y)), swap(bottom, high(x))]
        else:
            found[mask] = [swap(p, high(mask)) for p in found[mask ^ high(mask)]]
    for mask in range(1, senders, 2):
        found[mask] = [swap(p, 1) for p in found[mask ^ 1]]
    order = [(mask, low, a) for mask in range(senders) for low, a in found[mask]]
    return [(mask, low, a.shape[0]) for mask, low, a in order], [a for _, _, a in order]


def kernel(body, **options):
    return pl.pallas_call(body, **options)


def body(
    patch_states,
    queries,
    keys,
    values,
    out_proj,
    merge_gain,
    image_of_group,
    w_in,
    w_out,
    text_embeds,
    block_dest,
    placeholder_rows,
):
    row_count, feature_width = queries.shape
    members = lax.axis_size("vit")
    senders = lax.axis_size("dp")
    me = lax.axis_index("dp").astype(jnp.int32)[None]
    member = lax.axis_index("vit").astype(jnp.int32)
    heads = HEADS // members // GROUPS
    fold = fold_of(heads * HEAD_DIM)
    piece, packed_width = row_count // fold, heads * HEAD_DIM * fold
    vmem = pl.BlockSpec(memory_space=pltpu.VMEM)
    smem = pl.BlockSpec(memory_space=pltpu.SMEM)
    hbm = pl.BlockSpec(memory_space=pl.ANY)

    packed = kernel(
functools.partial(pack_kernel, members, GROUPS, fold),
        out_shape=[jax.ShapeDtypeStruct((3, piece, packed_width), jnp.bfloat16)]
        * (GROUPS * members),
        in_specs=[smem] + [vmem] * 3,
        out_specs=[vmem] * (GROUPS * members),
        scratch_shapes=[pltpu.VMEM((members, GROUPS, 3, piece, packed_width), jnp.bfloat16)],
    )(member[None], queries, keys, values)
    arrived = [
        [
            packed[g * members + s]
            if s == 0
            else shift(packed[g * members + s], s)
            for s in range(members)
        ]
        for g in range(GROUPS)
    ]

    image_ids = jnp.repeat(image_of_group[0], 4)
    shifts = lax.rem(member + members - jnp.arange(members, dtype=jnp.int32), members)
    image_ids = image_ids.reshape(members, row_count)[shifts].reshape(-1)
    blocks = block_dest.shape[1]
    block_height = row_count // 4 // blocks
    slots, text_rows = 2 * senders * block_height, text_embeds.shape[0]
    height = jnp.arange(block_height, dtype=jnp.int32)[None, :]
    destination = block_dest[0]
    positions = jnp.arange(blocks, dtype=jnp.int32)
    earlier = (destination[:, None] == destination[None, :]) & (
        positions[None, :] < positions[:, None]
    )
    slot_rank = jnp.sum(earlier.astype(jnp.int32), axis=1)
    slot_index = (destination ^ me) * 2 + slot_rank
    row_slots = (slot_index[:, None] * block_height + height).reshape(-1)
    selector = (jnp.arange(slots, dtype=jnp.int32)[:, None] == row_slots[None, :]).astype(
        jnp.bfloat16
    )
    others = jnp.arange(senders, dtype=jnp.int32) ^ me
    first_row = placeholder_rows.reshape(senders, 2)[others].reshape(-1)
    targets = jnp.where(first_row[:, None] >= 0, first_row[:, None] + height, -1).reshape(-1)
    placement = jnp.arange(text_rows, dtype=jnp.int32)[:, None] == targets[None, :]
    covered = jnp.any(placement, axis=1, keepdims=True).astype(jnp.int32)
    placement = placement.astype(jnp.bfloat16)

    ids_col, ids_row = image_ids[:, None], image_ids[None, :]
    returned = []
    for g in range(GROUPS):
        if g == GROUPS - 1:
            me, selector, placement, covered, ids_col, ids_row = lax.optimization_barrier(
                (me, selector, placement, covered, ids_col, ids_row)
            )
        attended = kernel(
functools.partial(attend_kernel, members, heads, fold),
            out_shape=[jax.ShapeDtypeStruct((piece, packed_width), jnp.bfloat16)] * members,
            in_specs=[vmem] * (2 + members),
            out_specs=[vmem] * members,
            scratch_shapes=[pltpu.VMEM((heads, row_count * members, LANES), jnp.bfloat16)] * 3,
            cost_estimate=pl.CostEstimate(
                flops=8 * heads * LANES * (row_count * members) ** 2,
                bytes_accessed=8 * row_count * feature_width,
                transcendentals=heads * (row_count * members) ** 2,
            ),
        )(ids_col, ids_row, *arrived[g])
        returned += [attended[s] if s == 0 else shift(attended[s], -s) for s in range(members)]

    half, merge_width = row_count // 8, 4 * feature_width
    above, below = kernel(
        functools.partial(project_kernel, members, GROUPS, fold),
        out_shape=[jax.ShapeDtypeStruct((half, merge_width), jnp.bfloat16)] * 2,
        in_specs=[smem] + [vmem] * (3 + GROUPS * members),
        out_specs=[vmem] * 2,
        scratch_shapes=[
            pltpu.VMEM((members, row_count, feature_width // members), jnp.bfloat16),
            pltpu.VMEM((feature_width // LANES, row_count, LANES), jnp.float32),
        ],
    )(member[None], patch_states, out_proj, merge_gain[None, :], *returned)

    rows = {("up", 0): above, ("low", 0): below}
    for step in range(1, members):
        above = ring(above, 1)
        below = ring(below, -1)
        rows["up", members - step] = above
        rows["low", step] = below
    late = [("up", 1), ("low", members - 1)]
    early = [name for name in rows if name not in late]

    units = w_out.shape[0] // LANES
    widths = [(units - max(1, units * 3 // 8)) * LANES, max(1, units * 3 // 8) * LANES]
    up_pieces, up_arrays = gather_pieces(w_in)
    down = [gather_pieces(w_out[: widths[0]]), gather_pieces(w_out[widths[0] :], direct=True)]
    hid = w_in.shape[1]

    def weight_cost(count, *parts):
        size = hid * senders * sum(parts)
        return pl.CostEstimate(flops=2 * count * size, bytes_accessed=2 * size, transcendentals=0)

    hidden = []
    for names in (early, late):
        count = len(names)
        hidden.append(
            kernel(
                functools.partial(hidden_kernel, up_pieces, count),
                out_shape=jax.ShapeDtypeStruct((count * half, hid), jnp.bfloat16),
                in_specs=[smem] + [vmem] * count + [hbm] * len(up_pieces),
                out_specs=vmem,
                scratch_shapes=[
                    pltpu.VMEM((senders, count * half, w_in.shape[0]), jnp.bfloat16),
                    pltpu.VMEM((senders,) + w_in.shape, jnp.bfloat16),
                    pltpu.VMEM((count * half, hid), jnp.float32),
                    pltpu.SemaphoreType.DMA((senders,)),
                ],
                cost_estimate=weight_cost(count * half, w_in.shape[0]),
            )(me, *[rows[name] for name in names], *up_arrays)
        )
    sums = [{}, {}]
    for c, given in ((0, (0,)), (0, (1,)), (1, (0, 1))):
        names = [(early, late)[at] for at in given]
        count = sum(map(len, names))
        wide, (pieces, arrays) = widths[c], down[c]
        results = kernel(
            functools.partial(sums_kernel, pieces, [len(each) for each in names]),
            out_shape=[jax.ShapeDtypeStruct((half, senders * wide), jnp.bfloat16)] * count,
            in_specs=[smem] + [vmem] * len(given) + [hbm] * len(pieces),
            out_specs=[vmem] * count,
            scratch_shapes=[
                pltpu.VMEM((count * half, hid), jnp.bfloat16),
                pltpu.VMEM((senders, wide, hid), jnp.bfloat16),
                pltpu.SemaphoreType.DMA((senders,)),
            ],
            cost_estimate=weight_cost(count * half, wide),
        )(me, *[hidden[at] for at in given], *arrays)
        sums[c].update(zip(sum(names, []), results))

    text = None
    for c, wide in enumerate(widths):
        width = senders * wide
        plus, minus = sums[c]["up", members - 1], sums[c]["low", 1]
        for step in range(1, members):
            if step > 1:
                plus = add(plus, sums[c]["up", members - step])
                minus = add(minus, sums[c]["low", step])
            plus = ring(plus, 1)
            minus = ring(minus, -1)
        each = 2 * block_height
        routed = kernel(
            route_kernel,
            out_shape=[jax.ShapeDtypeStruct((each, width), jnp.bfloat16)] * senders,
            in_specs=[vmem] * 5,
            out_specs=[vmem] * senders,
        )(selector, plus, sums[c]["up", 0], minus, sums[c]["low", 0])
        incoming = [routed[0]]
        for mask in range(1, senders):
            incoming.append(
                lax.ppermute(routed[mask], "dp", [(i, i ^ mask) for i in range(senders)])
            )
        before = [text] if c else []
        text = kernel(
            functools.partial(place_kernel, sum(widths[:c]), sum(widths), c > 0),
            out_shape=jax.ShapeDtypeStruct(text_embeds.shape, jnp.bfloat16),
            in_specs=[vmem, vmem, hbm] + [hbm] * len(before) + [vmem] * senders,
            out_specs=hbm,
            scratch_shapes=[
                pltpu.VMEM((slots, width), jnp.bfloat16),
                pltpu.VMEM((senders, text_rows, wide), jnp.bfloat16),
                pltpu.VMEM((senders, text_rows, wide), jnp.bfloat16),
                pltpu.SemaphoreType.DMA((senders,)),
                pltpu.SemaphoreType.DMA((senders,)),
            ],
            input_output_aliases={3: 0} if c else {},
        )(covered, placement, text_embeds, *before, *incoming)
    return text


def solution(mesh):
    placed = (
        P(("dp", "vit"), None),
        P(("dp", "vit"), None),
        P(("dp", "vit"), None),
        P(("dp", "vit"), None),
        P(),
        P(),
        P("dp", None),
        P("dp", "vit"),
        P("dp", "vit"),
        P(("dp", "vit"), None),
        P(("dp", "vit"), None),
        P(("dp", "vit"), None),
    )

    return jax.shard_map(
        body, mesh=mesh, in_specs=placed, out_specs=P(("dp", "vit"), None), check_vma=False
    )
```

```python
import functools

import jax
import jax.numpy as jnp
from jax import lax
from jax.experimental import pallas as pl
from jax.experimental.pallas import tpu as pltpu
from jax.sharding import PartitionSpec as P

HEADS = 16
HEAD_DIM = 80
EPSILON = 1e-06
LANES = 128
GROUPS = 2


def fold_of(width):
    fold = 1
    while (width * fold) % LANES:
        fold *= 2
    return fold


def pack_kernel(members, groups, fold, me_ref, q_ref, k_ref, v_ref, *refs):
    outs, buf = refs[:-1], refs[-1]
    rows, width = q_ref.shape
    part, piece = width // (members * groups), rows // fold
    for at, ref in enumerate((q_ref, k_ref, v_ref)):
        for member in range(members):
            for group in range(groups):
                low = (member * groups + group) * part
                for turn in range(fold):
                    buf[member, group, at, :, turn * part : (turn + 1) * part] = ref[
                        turn * piece : (turn + 1) * piece, low : low + part
                    ]
    for group in range(groups):
        for shift in range(members):
            outs[group * members + shift][...] = buf[lax.rem(me_ref[0] + shift, members), group]


def attend_kernel(members, heads, fold, ids_col_ref, ids_row_ref, *refs):
    packed, outs, (q_buf, k_buf, v_buf) = refs[:members], refs[members:-3], refs[-3:]
    _, piece, _ = packed[0].shape
    part, rows_each = heads * HEAD_DIM, piece * fold
    lane = lax.broadcasted_iota(jnp.int32, (piece, LANES - HEAD_DIM), 1)
    ones = jnp.where(lane == 0, 1.0, 0.0).astype(jnp.bfloat16)
    zeros = jnp.zeros((piece, LANES - HEAD_DIM), jnp.bfloat16)
    for head in range(heads):
        for turn in range(fold):
            low = turn * part + head * HEAD_DIM
            for at, ref in enumerate(packed):
                rows = slice((at * fold + turn) * piece, (at * fold + turn + 1) * piece)
                q_buf[head, rows, :HEAD_DIM] = ref[0, :, low : low + HEAD_DIM]
                k_buf[head, rows, :HEAD_DIM] = ref[1, :, low : low + HEAD_DIM]
                v_buf[head, rows, :HEAD_DIM] = ref[2, :, low : low + HEAD_DIM]
                q_buf[head, rows, HEAD_DIM:] = zeros
                k_buf[head, rows, HEAD_DIM:] = zeros
                v_buf[head, rows, HEAD_DIM:] = ones
    for at, out_ref in enumerate(outs):
        rows = slice(at * rows_each, (at + 1) * rows_each)
        allowed = ids_col_ref[rows, :] == ids_row_ref[...]
        for head in range(heads):
            scores = lax.dot_general(
                q_buf[head, rows, :],
                k_buf[head],
                (((1,), (1,)), ((), ())),
                preferred_element_type=jnp.float32,
            )
            scores = jnp.where(allowed, scores, -1e30)
            highest = jnp.max(scores, axis=-1, keepdims=True)
            weights = jnp.exp((scores - highest) * HEAD_DIM ** (-0.5)).astype(jnp.bfloat16)
            mixed = jnp.dot(weights, v_buf[head], preferred_element_type=jnp.float32)
            mixed = (mixed[:, :HEAD_DIM] / mixed[:, HEAD_DIM : HEAD_DIM + 1]).astype(jnp.bfloat16)
            for turn in range(fold):
                low = turn * part + head * HEAD_DIM
                out_ref[:, low : low + HEAD_DIM] = mixed[turn * piece : (turn + 1) * piece]


def project_kernel(members, groups, fold, me_ref, patch_ref, proj_ref, gain_ref, *refs):
    packed, (out_ref, rows_buf, normed) = refs[:-3], refs[-3:]
    piece, wide = packed[0].shape
    part = wide // fold
    depth = groups * part
    residual = patch_ref[...].astype(jnp.float32)
    for shift in range(members):
        for group in range(groups):
            for turn in range(fold):
                rows_buf[
                    shift, turn * piece : (turn + 1) * piece, group * part : (group + 1) * part
                ] = packed[group * members + shift][:, turn * part : (turn + 1) * part]
        low = pl.multiple_of(lax.rem(me_ref[0] + shift, members) * depth, depth)
        residual += jnp.dot(
            rows_buf[shift], proj_ref[pl.ds(low, depth), :], preferred_element_type=jnp.float32
        )
    mean_square = jnp.mean(residual * residual, axis=-1, keepdims=True)
    states = residual * lax.rsqrt(mean_square + EPSILON) * gain_ref[...]
    height, width = out_ref.shape[0], residual.shape[1]
    for tile in range(width // LANES):
        normed[tile] = states[:, tile * LANES : (tile + 1) * LANES]
    for at in range(4):
        for tile in range(width // LANES):
            columns = slice(at * width + tile * LANES, at * width + (tile + 1) * LANES)
            out_ref[:, columns] = normed[tile, pl.ds(at, height, stride=4), :].astype(jnp.bfloat16)


def hidden_kernel(pieces, count, me_ref, *refs):
    blocks, refs = refs[:count], refs[count:]
    given, (hidden_ref, rows_buf, up_buf, acc, sem) = refs[: len(pieces)], refs[len(pieces) :]
    fetch(pieces, given, up_buf, sem)
    members, _, depth = rows_buf.shape
    half = blocks[0].shape[0]
    for at, block in enumerate(blocks):
        for k in range(members):
            rows_buf[k, at * half : (at + 1) * half, :] = block[:, k * depth : (k + 1) * depth]
    acc[...] = jnp.zeros_like(acc)

    def one_piece(mask, carry):
        arrive(up_buf, sem, mask)
        acc[...] += jnp.dot(
            rows_buf[me_ref[0] ^ mask], up_buf[mask], preferred_element_type=jnp.float32
        )
        return carry

    lax.fori_loop(0, members, one_piece, 0)
    total = acc[...]
    hidden_ref[...] = (0.5 * total * (1.0 + lax.erf(total * 0.5**0.5))).astype(jnp.bfloat16)


def sums_kernel(pieces, counts, me_ref, *refs):
    given, refs = refs[: len(counts)], refs[len(counts) :]
    arrays, refs = refs[: len(pieces)], refs[len(pieces) :]
    sums, (hidden_buf, down_buf, down_sem) = refs[: sum(counts)], refs[sum(counts) :]
    fetch(pieces, arrays, down_buf, down_sem)
    low = 0
    for ref in given:
        hidden_buf[low : low + ref.shape[0]] = ref[...]
        low += ref.shape[0]
    contract(me_ref, hidden_buf, down_buf, down_sem, sums)


def fetch(pieces, refs, buf, sem):
    for (mask, low, length), ref in zip(pieces, refs):
        pltpu.make_async_copy(ref, buf.at[mask, pl.ds(low, length)], sem.at[mask]).start()


def arrive(buf, sem, mask):
    pltpu.make_async_copy(buf.at[mask], buf.at[mask], sem.at[mask]).wait()


def contract(me_ref, hidden_ref, down_buf, down_sem, sums):
    count, wide, _ = down_buf.shape
    half = sums[0].shape[0]

    def one_piece(mask, carry):
        arrive(down_buf, down_sem, mask)
        product = lax.dot_general(
            hidden_ref[...],
            down_buf[mask],
            (((1,), (1,)), ((), ())),
            preferred_element_type=jnp.float32,
        ).astype(jnp.bfloat16)
        low = pl.multiple_of((me_ref[0] ^ mask) * wide, wide)
        for at, ref in enumerate(sums):
            ref[:, pl.ds(low, wide)] = product[at * half : (at + 1) * half]
        return carry

    lax.fori_loop(0, count, one_piece, 0)


def route_kernel(selector_ref, come_ref, own_ref, *outs):
    merged = add(come_ref[...], own_ref[...])
    routed = jnp.dot(selector_ref[...], merged, preferred_element_type=jnp.float32).astype(
        jnp.bfloat16
    )
    each = outs[0].shape[0]
    for at, ref in enumerate(outs):
        ref[...] = routed[at * each : (at + 1) * each]


def line_up(arrived, rows_buf):
    each = arrived[0].shape[0]
    for at, ref in enumerate(arrived):
        rows_buf[at * each : (at + 1) * each, :] = ref[...]


def place_kernel(start, step, aliased, covered_ref, placement_ref, text_ref, *refs):
    refs = refs[1:] if aliased else refs
    arrived, (out_ref, rows_buf, before, result, in_sem, out_sem) = refs[:-6], refs[-6:]
    count, _, wide = before.shape

    def window(ref, at):
        return ref.at[:, pl.ds(at * step + start, wide)]

    reads = [
        pltpu.make_async_copy(window(text_ref, at), before.at[at], in_sem.at[at])
        for at in range(count)
    ]
    writes = [
        pltpu.make_async_copy(result.at[at], window(out_ref, at), out_sem.at[at])
        for at in range(count)
    ]
    for read in reads:
        read.start()
    line_up(arrived, rows_buf)
    covered = covered_ref[...] > 0
    for at in range(count):
        placed = jnp.dot(
            placement_ref[...],
            rows_buf[:, at * wide : (at + 1) * wide],
            preferred_element_type=jnp.float32,
        ).astype(jnp.bfloat16)
        reads[at].wait()
        result[at] = jnp.where(covered, placed, before[at])
        writes[at].start()
    for write in writes:
        write.wait()


def add(first, second):
    return (first.astype(jnp.float32) + second.astype(jnp.float32)).astype(jnp.bfloat16)


def ring(value, step):
    members = lax.axis_size("vit")
    return lax.ppermute(value, "vit", [(i, (i + step) % members) for i in range(members)])


def gather_pieces(value, direct=False):
    senders, rows = lax.axis_size("dp"), value.shape[0]
    side = 1
    while 2 * side * side < senders:
        side *= 2
    along_x, along_y = 2 * (side - 1), 2 * side * (side - 1)
    unit = 128 if rows >= 256 else 16
    cut = rows // 2 // unit * unit

    def swap(part, bit):
        low, array = part
        return low, lax.ppermute(array, "dp", [(i, i ^ bit) for i in range(senders)])

    def part_of(parts, top):
        if len(parts) == 2:
            return parts[0 if top else 1]
        array = parts[0][1]
        return (0, array[:cut]) if top else (cut, array[cut:])

    def high(mask):
        return 1 << (mask.bit_length() - 1)

    found = {0: [(0, value)]}
    for mask in range(2, senders, 2):
        x, y = mask & along_x, mask & along_y
        if x and y and direct:
            found[mask] = [swap(found[0][0], mask)]
        elif x and y:
            top = part_of(found[x | (y ^ high(y))], True)
            bottom = part_of(found[(x ^ high(x)) | y], False)
            found[mask] = [swap(top, high(y)), swap(bottom, high(x))]
        else:
            found[mask] = [swap(p, high(mask)) for p in found[mask ^ high(mask)]]
    for mask in range(1, senders, 2):
        found[mask] = [swap(p, 1) for p in found[mask ^ 1]]
    order = [(mask, low, a) for mask in range(senders) for low, a in found[mask]]
    return [(mask, low, a.shape[0]) for mask, low, a in order], [a for _, _, a in order]


def kernel(body, **options):
    return pl.pallas_call(body, **options)


def body(
    patch_states,
    queries,
    keys,
    values,
    out_proj,
    merge_gain,
    image_of_group,
    w_in,
    w_out,
    text_embeds,
    block_dest,
    placeholder_rows,
):
    row_count, feature_width = queries.shape
    members = lax.axis_size("vit")
    senders = lax.axis_size("dp")
    me = lax.axis_index("dp").astype(jnp.int32)[None]
    member = lax.axis_index("vit").astype(jnp.int32)
    heads = HEADS // members // GROUPS
    fold = fold_of(heads * HEAD_DIM)
    piece, packed_width = row_count // fold, heads * HEAD_DIM * fold
    vmem = pl.BlockSpec(memory_space=pltpu.VMEM)
    smem = pl.BlockSpec(memory_space=pltpu.SMEM)
    hbm = pl.BlockSpec(memory_space=pl.ANY)

    packed = kernel(
functools.partial(pack_kernel, members, GROUPS, fold),
        out_shape=[jax.ShapeDtypeStruct((3, piece, packed_width), jnp.bfloat16)]
        * (GROUPS * members),
        in_specs=[smem] + [vmem] * 3,
        out_specs=[vmem] * (GROUPS * members),
        scratch_shapes=[pltpu.VMEM((members, GROUPS, 3, piece, packed_width), jnp.bfloat16)],
    )(member[None], queries, keys, values)
    arrived = [
        [
            packed[g * members + s]
            if s == 0
            else ring(packed[g * members + s], s)
            for s in range(members)
        ]
        for g in range(GROUPS)
    ]

    image_ids = jnp.repeat(image_of_group[0], 4)
    shifts = lax.rem(member + members - jnp.arange(members, dtype=jnp.int32), members)
    image_ids = image_ids.reshape(members, row_count)[shifts].reshape(-1)
    blocks = block_dest.shape[1]
    block_height = row_count // 4 // blocks
    slots, text_rows = 2 * senders * block_height, text_embeds.shape[0]
    inside = jnp.arange(block_height, dtype=jnp.int32)[None, :]
    destination = block_dest[0]
    positions = jnp.arange(blocks, dtype=jnp.int32)
    earlier = (destination[:, None] == destination[None, :]) & (
        positions[None, :] < positions[:, None]
    )
    slot_rank = jnp.sum(earlier.astype(jnp.int32), axis=1)
    slot_index = (destination ^ me) * 2 + slot_rank
    row_slots = (slot_index[:, None] * block_height + inside).reshape(-1)
    selector = (jnp.arange(slots, dtype=jnp.int32)[:, None] == row_slots[None, :]).astype(
        jnp.bfloat16
    )
    others = jnp.arange(senders, dtype=jnp.int32) ^ me
    first_row = placeholder_rows.reshape(senders, 2)[others].reshape(-1)
    targets = jnp.where(first_row[:, None] >= 0, first_row[:, None] + inside, -1).reshape(-1)
    placement = jnp.arange(text_rows, dtype=jnp.int32)[:, None] == targets[None, :]
    covered = jnp.any(placement, axis=1, keepdims=True).astype(jnp.int32)
    placement = placement.astype(jnp.bfloat16)

    ids_col, ids_row = image_ids[:, None], image_ids[None, :]
    returned = []
    for g in range(GROUPS):
        if g == GROUPS - 1:
            me, selector, placement, covered, ids_col, ids_row = lax.optimization_barrier(
                (me, selector, placement, covered, ids_col, ids_row)
            )
        attended = kernel(
functools.partial(attend_kernel, members, heads, fold),
            out_shape=[jax.ShapeDtypeStruct((piece, packed_width), jnp.bfloat16)] * members,
            in_specs=[vmem] * (2 + members),
            out_specs=[vmem] * members,
            scratch_shapes=[pltpu.VMEM((heads, row_count * members, LANES), jnp.bfloat16)] * 3,
            cost_estimate=pl.CostEstimate(
                flops=8 * heads * LANES * (row_count * members) ** 2,
                bytes_accessed=8 * row_count * feature_width,
                transcendentals=heads * (row_count * members) ** 2,
            ),
        )(ids_col, ids_row, *arrived[g])
        returned += [attended[s] if s == 0 else ring(attended[s], -s) for s in range(members)]

    height, merge_width = row_count // 4, 4 * feature_width
    block = kernel(
        functools.partial(project_kernel, members, GROUPS, fold),
        out_shape=jax.ShapeDtypeStruct((height, merge_width), jnp.bfloat16),
        in_specs=[smem] + [vmem] * (3 + GROUPS * members),
        out_specs=vmem,
        scratch_shapes=[
            pltpu.VMEM((members, row_count, feature_width // members), jnp.bfloat16),
            pltpu.VMEM((feature_width // LANES, row_count, LANES), jnp.float32),
        ],
    )(member[None], patch_states, out_proj, merge_gain[None, :], *returned)

    rows = {0: block}
    for step in range(1, members):
        block = ring(block, 1)
        rows[members - step] = block
    late = [1]
    early = [name for name in rows if name not in late]

    units = w_out.shape[0] // LANES
    widths = [(units - max(1, units * 3 // 8)) * LANES, max(1, units * 3 // 8) * LANES]
    up_pieces, up_arrays = gather_pieces(w_in)
    down = [gather_pieces(w_out[: widths[0]]), gather_pieces(w_out[widths[0] :], direct=True)]
    hid = w_in.shape[1]

    def weight_cost(count, *parts):
        size = hid * senders * sum(parts)
        return pl.CostEstimate(flops=2 * count * size, bytes_accessed=2 * size, transcendentals=0)

    hidden = []
    for names in (early, late):
        count = len(names)
        hidden.append(
            kernel(
                functools.partial(hidden_kernel, up_pieces, count),
                out_shape=jax.ShapeDtypeStruct((count * height, hid), jnp.bfloat16),
                in_specs=[smem] + [vmem] * count + [hbm] * len(up_pieces),
                out_specs=vmem,
                scratch_shapes=[
                    pltpu.VMEM((senders, count * height, w_in.shape[0]), jnp.bfloat16),
                    pltpu.VMEM((senders,) + w_in.shape, jnp.bfloat16),
                    pltpu.VMEM((count * height, hid), jnp.float32),
                    pltpu.SemaphoreType.DMA((senders,)),
                ],
                cost_estimate=weight_cost(count * height, w_in.shape[0]),
            )(me, *[rows[name] for name in names], *up_arrays)
        )
    sums = [{}, {}]
    for c, given in ((0, (0,)), (0, (1,)), (1, (0, 1))):
        names = [(early, late)[at] for at in given]
        count = sum(map(len, names))
        wide, (pieces, arrays) = widths[c], down[c]
        results = kernel(
            functools.partial(sums_kernel, pieces, [len(each) for each in names]),
            out_shape=[jax.ShapeDtypeStruct((height, senders * wide), jnp.bfloat16)] * count,
            in_specs=[smem] + [vmem] * len(given) + [hbm] * len(pieces),
            out_specs=[vmem] * count,
            scratch_shapes=[
                pltpu.VMEM((count * height, hid), jnp.bfloat16),
                pltpu.VMEM((senders, wide, hid), jnp.bfloat16),
                pltpu.SemaphoreType.DMA((senders,)),
            ],
            cost_estimate=weight_cost(count * height, wide),
        )(me, *[hidden[at] for at in given], *arrays)
        sums[c].update(zip(sum(names, []), results))

    text = None
    for c, wide in enumerate(widths):
        width = senders * wide
        way = 1 if c == 0 else -1
        total = sums[c][-way % members]
        for step in range(1, members):
            if step > 1:
                total = add(total, sums[c][-way * step % members])
            total = ring(total, way)
        each = 2 * block_height
        routed = kernel(
            route_kernel,
            out_shape=[jax.ShapeDtypeStruct((each, width), jnp.bfloat16)] * senders,
            in_specs=[vmem] * 3,
            out_specs=[vmem] * senders,
        )(selector, total, sums[c][0])
        incoming = [routed[0]]
        for mask in range(1, senders):
            incoming.append(
                lax.ppermute(routed[mask], "dp", [(i, i ^ mask) for i in range(senders)])
            )
        before = [text] if c else []
        text = kernel(
            functools.partial(place_kernel, sum(widths[:c]), sum(widths), c > 0),
            out_shape=jax.ShapeDtypeStruct(text_embeds.shape, jnp.bfloat16),
            in_specs=[vmem, vmem, hbm] + [hbm] * len(before) + [vmem] * senders,
            out_specs=hbm,
            scratch_shapes=[
                pltpu.VMEM((slots, width), jnp.bfloat16),
                pltpu.VMEM((senders, text_rows, wide), jnp.bfloat16),
                pltpu.VMEM((senders, text_rows, wide), jnp.bfloat16),
                pltpu.SemaphoreType.DMA((senders,)),
                pltpu.SemaphoreType.DMA((senders,)),
            ],
            input_output_aliases={3: 0} if c else {},
        )(covered, placement, text_embeds, *before, *incoming)
    return text


def solution(mesh):
    placed = (
        P(("dp", "vit"), None),
        P(("dp", "vit"), None),
        P(("dp", "vit"), None),
        P(("dp", "vit"), None),
        P(),
        P(),
        P("dp", None),
        P("dp", "vit"),
        P("dp", "vit"),
        P(("dp", "vit"), None),
        P(("dp", "vit"), None),
        P(("dp", "vit"), None),
    )

    return jax.shard_map(
        body, mesh=mesh, in_specs=placed, out_specs=P(("dp", "vit"), None), check_vma=False
    )
```
